32 devices in a mesh: clip: 4 (over z), frame: 2 (over y), head: 4 (over x, core).
Axes of the slice: x: 2, y: 2, z: 4, core: 2. Of those that a mesh axis runs over, the one named last changes fastest.
Arguments:
- tokens: float32 [4, 16, 256, 1152], P('clip', 'frame'), may hold values from -6 to 6
- condition: float32 [4, 1152], P(None, ('clip', 'frame')), may hold values from -6 to 6
- w_qkv: float32 [2, 1152, 3, 1152], P(None, ('clip', 'frame'), None, 'head'), may hold values from -0.1875 to 0.1875
- b_qv: float32 [2, 2, 1152], P(None, None, 'head'), may hold values from -3 to 3
- w_out: float32 [2, 1152, 1152], P(None, 'head', ('clip', 'frame')), may hold values from -0.5 to 0.5
- b_out: float32 [2, 1152], replicated, may hold values from -2 to 2
- w_up: float32 [2, 1152, 4608], P(None, ('clip', 'frame'), 'head'), may hold values from -0.1875 to 0.1875
- b_up: float32 [2, 4608], P(None, 'head'), may hold values from -3 to 3
- w_down: float32 [2, 4608, 1152], P(None, 'head', ('clip', 'frame')), may hold values from -0.09375 to 0.09375
- b_down: float32 [2, 1152], replicated, may hold values from -2 to 2
- w_mod: float32 [2, 1152, 6, 1152], P(None, ('clip', 'frame'), None, 'head'), may hold values from -0.1875 to 0.1875
- b_mod: float32 [2, 6, 1152], replicated, may hold values from -2 to 2
- out_grad: float32 [4, 16, 256, 1152], P('clip', 'frame'), may hold values from -6 to 6
Outputs:
- result: float32 [4, 16, 256, 1152], P('clip', 'frame')
- tokens_grad: float32 [4, 16, 256, 1152], P('clip', 'frame')
- cond_grad: float32 [4, 1152], P(None, ('clip', 'frame'))
- w_qkv_grad: float32 [2, 1152, 3, 1152], P(None, ('clip', 'frame'), None, 'head')
- b_qv_grad: float32 [2, 2, 1152], P(None, None, 'head')
- w_out_grad: float32 [2, 1152, 1152], P(None, 'head', ('clip', 'frame'))
- b_out_grad: float32 [2, 1152], replicated
- w_up_grad: float32 [2, 1152, 4608], P(None, ('clip', 'frame'), 'head')
- b_up_grad: float32 [2, 4608], P(None, 'head')
- w_down_grad: float32 [2, 4608, 1152], P(None, 'head', ('clip', 'frame'))
- b_down_grad: float32 [2, 1152], replicated
- w_mod_grad: float32 [2, 1152, 6, 1152], P(None, ('clip', 'frame'), None, 'head')
- b_mod_grad: float32 [2, 6, 1152], replicated
The draws below stay inside these ranges and needn't reach their ends.
All inputs are finite; a program needn't handle non-finite values.
Results may differ from the reference program's by a relative error of at most 0.024.
Values may be sent and summed in bfloat16 or wider, within the bound.
No kernel may reach another device: no remote copies, remote signals or barrier semaphores. Data moves between devices by JAX's collectives and lax.ppermute only.
A program may use at most 320 MiB of HBM per device.

```python
import jax
import jax.numpy as jnp
from jax import lax

D = 1152
HEADS = 16
HEAD_DIM = 72
FF = 4608
PLACES = 256
LAYERS = 2
FRAMES = 16
CLIPS = 4


def block_levels(stream_key, dims, cuts, smallest, high):
    def one(position, blocks):
        draws = jax.random.uniform(jax.random.fold_in(jax.random.fold_in(stream_key, 6), position), (blocks,), jnp.float32, smallest / len(cuts), high / len(cuts))
        return jnp.repeat(jnp.exp(draws), dims[position] // blocks).reshape((-1,) + (1,) * (len(dims) - position - 1))

    loudness = one(*cuts[0])
    for cut in cuts[1:]:
        loudness = loudness * one(*cut)
    return loudness


def noise(own_key, dims, scale, bound, cuts=(), held_as=jnp.bfloat16):
    loudness = block_levels(own_key, dims, cuts, -0.22, 0.18) if cuts else 1.0
    drawn = jax.random.normal(own_key, dims, jnp.float32) * scale * loudness
    return jnp.minimum(jnp.maximum(drawn, -bound), bound).astype(held_as)


def setup_inputs(seed: int = 0) -> dict:
    arg_keys = jax.random.split(jax.random.key(seed), 14)
    tokens = noise(arg_keys[0], (CLIPS, FRAMES, PLACES, D), 1.0, 6.0, ((0, 4), (1, 2)), jnp.float32)
    condition = noise(arg_keys[1], (CLIPS, D), 1.0, 6.0, ((1, 8),), jnp.float32)
    w_qkv = noise(arg_keys[2], (LAYERS, D, 3, D), D ** -0.5, 0.1875, ((1, 8), (3, 4)), jnp.float32)
    b_qv = noise(arg_keys[3], (LAYERS, 2, D), 0.5, 3.0, ((2, 4),), jnp.float32)
    w_out = noise(arg_keys[4], (LAYERS, D, D), (D // 8) ** -0.5, 0.5, ((1, 4), (2, 8)), jnp.float32)
    b_out = noise(arg_keys[5], (LAYERS, D), 0.3, 2.0, (), jnp.float32)
    w_up = noise(arg_keys[6], (LAYERS, D, FF), D ** -0.5, 0.1875, ((1, 8), (2, 4)), jnp.float32)
    b_up = noise(arg_keys[7], (LAYERS, FF), 0.5, 3.0, ((1, 4),), jnp.float32)
    w_down = noise(arg_keys[8], (LAYERS, FF, D), FF ** -0.5, 0.09375, ((1, 4), (2, 8)), jnp.float32)
    b_down = noise(arg_keys[9], (LAYERS, D), 0.3, 2.0, (), jnp.float32)
    w_mod = noise(arg_keys[10], (LAYERS, D, 6, D), D ** -0.5, 0.1875, ((1, 8), (3, 4)), jnp.float32)
    b_mod = noise(arg_keys[11], (LAYERS, 6, D), 0.3, 2.0, (), jnp.float32)
    out_grad = noise(arg_keys[12], (CLIPS, FRAMES, PLACES, D), 1.0, 6.0, ((0, 4), (1, 2)), jnp.float32)
    return {"tokens": tokens, "condition": condition, "w_qkv": w_qkv, "b_qv": b_qv, "w_out": w_out, "b_out": b_out, "w_up": w_up, "b_up": b_up, "w_down": w_down, "b_down": b_down, "w_mod": w_mod, "b_mod": b_mod, "out_grad": out_grad}


highest = lax.Precision.HIGHEST

@jax.custom_vjp
def low(v):
    return lax.optimization_barrier(v.astype(jnp.bfloat16)).astype(jnp.float32)

@jax.custom_vjp
def low_back(v):
    return v

def low_keep(v):
    return (low(v), None)

def low_pass(kept, grad):
    return (grad,)

def back_keep(v):
    return (v, None)

def back_low(kept, grad):
    return (low(grad),)
low.defvjp(low_keep, low_pass)
low_back.defvjp(back_keep, back_low)

def normalize(value):
    center = value - lax.optimization_barrier(jnp.mean(value, axis=-1, keepdims=True))
    inverse = lax.rsqrt(lax.optimization_barrier(jnp.mean(center * center, axis=-1, keepdims=True)) + 1e-06)
    return center * inverse

def gelu_tanh(value):
    inner = 0.7978845608028654 * (value + 0.044715 * value * value * value)
    return 0.5 * value * (1.0 + jnp.tanh(inner))

def attend(query, keys, values, across):
    if across:
        first = 'fpnk,gpnk->pnfg'
        second = 'pnfg,gpnk->fpnk'
    else:
        first = 'fpnk,fqnk->fnpq'
        second = 'fnpq,fqnk->fpnk'
    scores = low_back(jnp.einsum(first, query, keys, precision=highest) * HEAD_DIM ** (-0.5))
    probs = low(jax.nn.softmax(scores, axis=-1))
    return jnp.einsum(second, probs, values, precision=highest)

def layer(inputs, shifts, weights, biases, across):
    w_query, w_project, w_expand, w_reduce = weights
    bias_qv, bias_out, bias_up, bias_down = biases
    frames = inputs.shape[0]
    places = inputs.shape[1]
    mixed_one = low(normalize(inputs) * (1.0 + shifts[1]) + shifts[0])
    joined = jnp.einsum('fpd,dje->fpje', mixed_one, w_query, precision=highest)
    bias_full = jnp.stack([bias_qv[0], jnp.zeros_like(bias_qv[0]), bias_qv[1]])
    triple = low(low_back(joined + bias_full)).reshape(frames, places, 3, HEADS, HEAD_DIM)
    attended = attend(triple[:, :, 0], triple[:, :, 1], triple[:, :, 2], across)
    attended = low(low_back(attended.reshape(frames, places, D)))
    branch_one = low_back(jnp.einsum('fpe,ed->fpd', attended, w_project, precision=highest))
    middle = inputs + shifts[2] * (branch_one + bias_out)
    mixed_two = low(normalize(middle) * (1.0 + shifts[4]) + shifts[3])
    hidden = low_back(jnp.einsum('fpd,dh->fph', mixed_two, w_expand, precision=highest) + bias_up)
    activated = low(gelu_tanh(hidden))
    branch_two = low_back(jnp.einsum('fph,hd->fpd', activated, w_reduce, precision=highest))
    return middle + shifts[5] * (branch_two + bias_down)

def forward(tokens, condition, w_qkv, b_qv, w_out, b_out, w_up, b_up, w_down, b_down, w_mod, b_mod):
    modulation = jnp.einsum('cd,ldje->lcje', jax.nn.silu(condition), w_mod, precision=highest) + b_mod[:, None]
    copies = (low(w_qkv), low(w_out), low(w_up), low(w_down))

    def clip_step(carry, pieces):
        inputs, shifts = pieces
        for layer_index in range(LAYERS):
            weights = (copies[0][layer_index], copies[1][layer_index], copies[2][layer_index], copies[3][layer_index])
            biases = (b_qv[layer_index], b_out[layer_index], b_up[layer_index], b_down[layer_index])
            inputs = layer(inputs, shifts[layer_index], weights, biases, layer_index % 2 == 1)
        return (carry, inputs)
    start = jnp.zeros((), jnp.float32)
    _, outputs = lax.scan(jax.checkpoint(clip_step), start, (tokens, jnp.swapaxes(modulation, 0, 1)))
    return outputs

def reference(tokens, condition, w_qkv, b_qv, w_out, b_out, w_up, b_up, w_down, b_down, w_mod, b_mod, out_grad):
    result, pull = jax.vjp(forward, tokens, condition, w_qkv, b_qv, w_out, b_out, w_up, b_up, w_down, b_down, w_mod, b_mod)
    grads = pull(out_grad)
    return (result, grads[0], grads[1], grads[2], grads[3], grads[4], grads[5], grads[6], grads[7], grads[8], grads[9], grads[10], grads[11])
```

```python
import functools

import jax
import jax.numpy as jnp
from jax import lax
from jax.experimental import pallas as pl
from jax.experimental.pallas import tpu as pltpu
from jax.sharding import PartitionSpec as P

HEAD_DIM = 72


highest = lax.Precision.HIGHEST


def normalize(value):
    center = value - jnp.mean(value, axis=-1, keepdims=True)
    inverse = lax.rsqrt(jnp.mean(center * center, axis=-1, keepdims=True) + 1e-06)
    return (center * inverse, inverse)


def norm_back(grad, normed, inverse):
    first_mean = jnp.mean(grad, axis=-1, keepdims=True)
    second_mean = jnp.mean(grad * normed, axis=-1, keepdims=True)
    return inverse * (grad - first_mean - normed * second_mean)


def gelu_tanh(value):
    inner = 0.7978845608028654 * (value + 0.044715 * value * value * value)
    return 0.5 * value * (1.0 + jnp.tanh(inner))


def gelu_slope(value):
    inner = 0.7978845608028654 * (value + 0.044715 * value * value * value)
    tangent = jnp.tanh(inner)
    return 0.5 * (1.0 + tangent) + 0.5 * value * (1.0 - tangent * tangent) * 0.7978845608028654 * (
        1.0 + 3.0 * 0.044715 * value * value
    )


def score_specs(across):
    if across:
        return ("cabnk,cebnk->cbnae", "cbnae,cebnk->cabnk", "cbnae,cabnk->cebnk")
    return ("cabnk,caenk->canbe", "canbe,caenk->cabnk", "canbe,cabnk->caenk")


def branch_total(partial_value):
    share = lax.psum_scatter(
        partial_value.astype(jnp.bfloat16), "head", scatter_dimension=3, tiled=True
    ).astype(jnp.float32)
    return lax.all_gather(share.astype(jnp.bfloat16), "head", axis=3, tiled=True).astype(
        share.dtype
    )


def head_total(partial_value):
    share = lax.psum_scatter(
        partial_value.astype(jnp.bfloat16), "head", scatter_dimension=3, tiled=True
    ).astype(jnp.float32)
    return lax.all_gather(share.astype(jnp.bfloat16), "head", axis=3, tiled=True).astype(
        share.dtype
    )


def layer_forward(inputs, shifts, weights, biases, across):
    w_query, w_project, w_expand, w_reduce = weights
    bias_qv, bias_out, bias_up, bias_down = biases
    shape = inputs.shape
    width = w_query.shape[2]
    heads = width // HEAD_DIM
    first, second, third = score_specs(across)
    normed_one, inverse_one = normalize(inputs)
    mixed_one = (normed_one * (1.0 + shifts[1]) + shifts[0]).astype(jnp.bfloat16)
    joined = jnp.einsum("cabd,dje->cabje", mixed_one, w_query, preferred_element_type=jnp.float32)
    bias_full = jnp.stack([bias_qv[0], jnp.zeros_like(bias_qv[0]), bias_qv[1]])
    triple = (joined + bias_full).astype(jnp.bfloat16).reshape(shape[:3] + (3, heads, HEAD_DIM))
    query = triple[:, :, :, 0]
    keys = triple[:, :, :, 1]
    values = triple[:, :, :, 2]
    scores = jnp.einsum(first, query, keys, preferred_element_type=jnp.float32) * HEAD_DIM ** (-0.5)
    highest_score = jnp.max(scores, axis=-1, keepdims=True)
    expanded = jnp.exp(scores - highest_score)
    total = jnp.sum(expanded, axis=-1, keepdims=True)
    log_total = highest_score + jnp.log(total)
    soft_low = (expanded / total).astype(jnp.bfloat16)
    attended = jnp.einsum(second, soft_low, values, preferred_element_type=jnp.float32)
    attended = attended.astype(jnp.bfloat16).reshape(shape[:3] + (width,))
    partial_value = jnp.einsum(
        "cabe,ed->cabd", attended, w_project, preferred_element_type=jnp.float32
    )
    branch_one = branch_total(partial_value)
    middle = inputs + shifts[2] * (branch_one + bias_out)
    normed_two, inverse_two = normalize(middle)
    mixed_two = (normed_two * (1.0 + shifts[4]) + shifts[3]).astype(jnp.bfloat16)
    hidden = (
        jnp.einsum("cabd,df->cabf", mixed_two, w_expand, preferred_element_type=jnp.float32)
        + bias_up
    )
    activated = gelu_tanh(hidden).astype(jnp.bfloat16)
    partial_two = jnp.einsum(
        "cabf,fd->cabd", activated, w_reduce, preferred_element_type=jnp.float32
    )
    branch_two = branch_total(partial_two)
    output = middle + shifts[5] * (branch_two + bias_down)
    saved = (
        normed_one,
        inverse_one,
        mixed_one,
        query,
        keys,
        values,
        log_total,
        attended,
        branch_one,
        normed_two,
        inverse_two,
        mixed_two,
        hidden,
        activated,
        branch_two,
    )
    return (output, saved)


def layer_backward(grad_out, saved, shifts, weights, biases, across):
    (
        normed_one,
        inverse_one,
        mixed_one,
        query,
        keys,
        values,
        log_total,
        attended,
        branch_one,
        normed_two,
        inverse_two,
        mixed_two,
        hidden,
        activated,
        branch_two,
    ) = saved
    w_query, w_project, w_expand, w_reduce = weights
    bias_qv, bias_out, bias_up, bias_down = biases
    shape = grad_out.shape
    width = w_query.shape[2]
    first, second, third = score_specs(across)
    token_axes = (1, 2)
    every_axis = (0, 1, 2)
    dgate_two = jnp.sum(grad_out * (branch_two + bias_down), axis=token_axes)
    scaled_two = shifts[5] * grad_out
    grad_bias_down = jnp.sum(scaled_two, axis=every_axis)
    scaled_two_low = scaled_two.astype(jnp.bfloat16)
    grad_reduce = jnp.einsum(
        "cabf,cabd->fd", activated, scaled_two_low, preferred_element_type=jnp.float32
    )
    grad_active = jnp.einsum(
        "cabd,fd->cabf", scaled_two_low, w_reduce, preferred_element_type=jnp.float32
    )
    grad_hidden = (grad_active * gelu_slope(hidden)).astype(jnp.bfloat16)
    grad_bias_up = jnp.sum(grad_hidden, axis=every_axis, dtype=jnp.float32)
    grad_expand = jnp.einsum(
        "cabd,cabf->df", mixed_two, grad_hidden, preferred_element_type=jnp.float32
    )
    grad_mixed_two = head_total(
        jnp.einsum("cabf,df->cabd", grad_hidden, w_expand, preferred_element_type=jnp.float32)
    )
    dshift_two = jnp.sum(grad_mixed_two, axis=token_axes)
    dscale_two = jnp.sum(grad_mixed_two * normed_two, axis=token_axes)
    grad_middle = grad_out + norm_back(grad_mixed_two * (1.0 + shifts[4]), normed_two, inverse_two)
    dgate_one = jnp.sum(grad_middle * (branch_one + bias_out), axis=token_axes)
    scaled_one = shifts[2] * grad_middle
    grad_bias_out = jnp.sum(scaled_one, axis=every_axis)
    scaled_one_low = scaled_one.astype(jnp.bfloat16)
    grad_project = jnp.einsum(
        "cabe,cabd->ed", attended, scaled_one_low, preferred_element_type=jnp.float32
    )
    grad_attended = jnp.einsum(
        "cabd,ed->cabe", scaled_one_low, w_project, preferred_element_type=jnp.float32
    )
    grad_attended = grad_attended.astype(jnp.bfloat16).reshape(query.shape)
    scores = jnp.einsum(first, query, keys, preferred_element_type=jnp.float32) * HEAD_DIM ** (-0.5)
    probs = jnp.exp(scores - log_total)
    grad_probs = jnp.einsum(first, grad_attended, values, preferred_element_type=jnp.float32)
    grad_values = jnp.einsum(
        third, probs.astype(jnp.bfloat16), grad_attended, preferred_element_type=jnp.float32
    )
    mean_term = jnp.sum(grad_probs * probs, axis=-1, keepdims=True)
    grad_scores = (probs * (grad_probs - mean_term)).astype(jnp.bfloat16)
    grad_query = jnp.einsum(
        second, grad_scores, keys, preferred_element_type=jnp.float32
    ) * HEAD_DIM ** (-0.5)
    grad_keys = jnp.einsum(
        third, grad_scores, query, preferred_element_type=jnp.float32
    ) * HEAD_DIM ** (-0.5)
    grad_triple = jnp.stack([grad_query, grad_keys, grad_values], axis=3).astype(jnp.bfloat16)
    grad_triple = grad_triple.reshape(shape[:3] + (3, width))
    grad_bias_qv = jnp.sum(grad_triple[:, :, :, 0::2], axis=every_axis, dtype=jnp.float32)
    grad_query_weight = jnp.einsum(
        "cabd,cabje->dje", mixed_one, grad_triple, preferred_element_type=jnp.float32
    )
    grad_mixed_one = head_total(
        jnp.einsum("cabje,dje->cabd", grad_triple, w_query, preferred_element_type=jnp.float32)
    )
    dshift_one = jnp.sum(grad_mixed_one, axis=token_axes)
    dscale_one = jnp.sum(grad_mixed_one * normed_one, axis=token_axes)
    grad_inputs = grad_middle + norm_back(
        grad_mixed_one * (1.0 + shifts[1]), normed_one, inverse_one
    )
    grad_shifts = jnp.stack(
        [dshift_one, dscale_one, dgate_one, dshift_two, dscale_two, dgate_two], axis=1
    )
    weight_grads = (grad_query_weight, grad_project, grad_expand, grad_reduce)
    bias_grads = (grad_bias_qv, grad_bias_out, grad_bias_up, grad_bias_down)
    return (grad_inputs, grad_shifts, weight_grads, bias_grads)


def body(
    tokens, condition, w_qkv, b_qv, w_out, b_out, w_up, b_up, w_down, b_down, w_mod, b_mod, out_grad
):
    clip_count = tokens.shape[0]
    columns = w_mod.shape[3]
    head_start = lax.axis_index("head") * columns
    clip_start = lax.axis_index("clip") * clip_count
    activated_cond = jax.nn.silu(condition)
    partial_value = jnp.einsum("cd,ldje->lcje", activated_cond, w_mod, precision=highest)
    spread = jnp.zeros(partial_value.shape[:3] + (columns * lax.axis_size("head"),), jnp.float32)
    spread = lax.dynamic_update_slice_in_dim(spread, partial_value, head_start, 3)
    modulation = lax.psum(spread, ("clip", "frame", "head")) + b_mod[:, None]
    own = lax.dynamic_slice_in_dim(modulation, clip_start, clip_count, 1)
    factors = own[:, :, :, None, None, :]
    shifts_first = [factors[0, :, index] for index in range(6)]
    shifts_second = [factors[1, :, index] for index in range(6)]
    biases_first = (b_qv[0], b_out[0], b_up[0], b_down[0])
    biases_second = (b_qv[1], b_out[1], b_up[1], b_down[1])

    def gather_copies(layer_index):
        return (
            lax.all_gather(
                w_qkv[layer_index].astype(jnp.bfloat16), ("clip", "frame"), axis=0, tiled=True
            ),
            lax.all_gather(
                w_out[layer_index].astype(jnp.bfloat16), ("clip", "frame"), axis=1, tiled=True
            ),
            lax.all_gather(
                w_up[layer_index].astype(jnp.bfloat16), ("clip", "frame"), axis=0, tiled=True
            ),
            lax.all_gather(
                w_down[layer_index].astype(jnp.bfloat16), ("clip", "frame"), axis=1, tiled=True
            ),
        )

    def regather(layer_index):
        return (
            lax.all_gather(
                w_qkv[layer_index].astype(jnp.bfloat16), ("clip", "frame"), axis=0, tiled=True
            ),
            lax.all_gather(
                w_out[layer_index].astype(jnp.bfloat16), ("clip", "frame"), axis=1, tiled=True
            ),
            lax.all_gather(
                w_up[layer_index].astype(jnp.bfloat16), ("clip", "frame"), axis=0, tiled=True
            ),
            lax.all_gather(
                w_down[layer_index].astype(jnp.bfloat16), ("clip", "frame"), axis=1, tiled=True
            ),
        )

    def return_grads(grads):
        return (
            lax.psum_scatter(grads[0], ("clip", "frame"), scatter_dimension=0, tiled=True),
            lax.psum_scatter(grads[1], ("clip", "frame"), scatter_dimension=1, tiled=True),
            lax.psum_scatter(grads[2], ("clip", "frame"), scatter_dimension=0, tiled=True),
            lax.psum_scatter(grads[3], ("clip", "frame"), scatter_dimension=1, tiled=True),
        )

    first_weights = gather_copies(0)
    middle, first_saved = layer_forward(tokens, shifts_first, first_weights, biases_first, False)
    placed = lax.all_to_all(
        middle.astype(jnp.bfloat16), "frame", split_axis=2, concat_axis=1, tiled=True
    ).astype(middle.dtype)
    second_weights = gather_copies(1)
    final, second_saved = layer_forward(placed, shifts_second, second_weights, biases_second, True)
    result = lax.all_to_all(
        final.astype(jnp.bfloat16), "frame", split_axis=1, concat_axis=2, tiled=True
    ).astype(final.dtype)
    second_weights = regather(1)
    grad_placed = lax.all_to_all(
        out_grad.astype(jnp.bfloat16), "frame", split_axis=2, concat_axis=1, tiled=True
    ).astype(out_grad.dtype)
    grad_second, mod_second, wgrad_second, bgrad_second = layer_backward(
        grad_placed, second_saved, shifts_second, second_weights, biases_second, True
    )
    shard_second = return_grads(wgrad_second)
    grad_middle = lax.all_to_all(
        grad_second.astype(jnp.bfloat16), "frame", split_axis=1, concat_axis=2, tiled=True
    ).astype(grad_second.dtype)
    first_weights = regather(0)
    tokens_grad, mod_first, wgrad_first, bgrad_first = layer_backward(
        grad_middle, first_saved, shifts_first, first_weights, biases_first, False
    )
    shard_first = return_grads(wgrad_first)
    stacked_mod = jnp.stack([mod_first, mod_second])
    placed_mod = lax.dynamic_update_slice_in_dim(
        jnp.zeros_like(modulation), stacked_mod, clip_start, 1
    )
    total_mod, total_qv, total_out, total_up, total_down = lax.psum(
        (
            placed_mod,
            jnp.stack([bgrad_first[0], bgrad_second[0]]),
            jnp.stack([bgrad_first[1], bgrad_second[1]]),
            jnp.stack([bgrad_first[2], bgrad_second[2]]),
            jnp.stack([bgrad_first[3], bgrad_second[3]]),
        ),
        ("clip", "frame"),
    )
    b_mod_grad = jnp.sum(total_mod, axis=1)
    mod_columns = lax.dynamic_slice_in_dim(total_mod, head_start, columns, 3)
    w_mod_grad = jnp.einsum("cd,lcje->ldje", activated_cond, mod_columns, precision=highest)
    cond_part = jnp.einsum("lcje,ldje->cd", mod_columns, w_mod, precision=highest)
    cond_total = lax.psum(cond_part, "head")
    sigma = jax.nn.sigmoid(condition)
    cond_grad = cond_total * sigma * (1.0 + condition * (1.0 - sigma))
    w_qkv_grad = jnp.stack([shard_first[0], shard_second[0]])
    w_out_grad = jnp.stack([shard_first[1], shard_second[1]])
    w_up_grad = jnp.stack([shard_first[2], shard_second[2]])
    w_down_grad = jnp.stack([shard_first[3], shard_second[3]])
    return (
        result,
        tokens_grad,
        cond_grad,
        w_qkv_grad,
        total_qv,
        w_out_grad,
        total_out,
        w_up_grad,
        total_up,
        w_down_grad,
        total_down,
        w_mod_grad,
        b_mod_grad,
    )


BF = jnp.bfloat16
F32 = jnp.float32
PART = 384
HALF = 512
BLOCK = 256
VMEM_LIMIT = 60 * 1024 * 1024
GATHER_ORDERS = (("zxy", "zyx", "xzy"), ("zyx", "zxy", "yzx"))
SCATTER_ORDERS = (("yxz", "xyz", "yzx"), ("xyz", "yxz", "xzy"))


def nn(a, b):
    return lax.dot_general(a, b, (((1,), (0,)), ((), ())), preferred_element_type=F32)


def nt(a, b):
    return lax.dot_general(a, b, (((1,), (1,)), ((), ())), preferred_element_type=F32)


def tn(a, b):
    return lax.dot_general(a, b, (((0,), (0,)), ((), ())), preferred_element_type=F32)


def xor_pairs(size, bit):
    return [(i, i ^ bit) for i in range(size)]


def swap_core(value):
    return lax.ppermute(value, "head", xor_pairs(4, 1))


def swap_x(value):
    return lax.ppermute(value, "head", xor_pairs(4, 2))


def swap_y(value):
    return lax.ppermute(value, "frame", xor_pairs(2, 1))


def swap_z(value, bit):
    return lax.ppermute(value, "clip", xor_pairs(4, bit))


def swap_clip(value, bit):
    return lax.ppermute(value, ("frame", "head"), xor_pairs(8, bit))


def params(steps=1, **extra):
    return pltpu.CompilerParams(
        dimension_semantics=("arbitrary",) * steps, vmem_limit_bytes=VMEM_LIMIT, **extra
    )


def cost(flops, moved, exps=0):
    return pl.CostEstimate(flops=int(flops), bytes_accessed=int(moved), transcendentals=int(exps))


def shape_of(shape, dtype):
    return jax.ShapeDtypeStruct(tuple(shape), dtype)


def gather_part(shard, order):
    current = shard
    for axis in order[:2]:
        if axis == "z":
            current = jnp.stack([current] + [swap_z(current, k) for k in (1, 2, 3)])
        else:
            current = jnp.stack([current, (swap_x if axis == "x" else swap_y)(current)])
    return (current, (swap_x if order[2] == "x" else swap_y)(current))


def gather_buffer(shard, orders):
    found = []
    for index, order in enumerate(orders):
        found.extend(gather_part(shard[:, index * PART : (index + 1) * PART], order))
    return found


def weight_copies(refs, orders, place, rows, target, sems):
    z, y = place
    copies = []
    for index, order in enumerate(orders):
        sizes = {"x": 2, "y": 2, "z": 4}
        for last in range(2):
            for outer in range(sizes[order[1]]):
                for inner in range(sizes[order[0]]):
                    at = {order[2]: last, order[1]: outer, order[0]: inner}
                    start = ((at["z"] ^ z) * 2 + (at["y"] ^ y)) * rows
                    copies.append(
                        pltpu.make_async_copy(
                            refs[2 * index + last].at[outer, inner],
                            target.at[
                                at["x"],
                                pl.ds(pl.multiple_of(start, 16), rows),
                                pl.ds(index * PART, PART),
                            ],
                            sems.at[len(copies)],
                        )
                    )
    return copies


ANY_SPEC = pl.BlockSpec(memory_space=pl.ANY)


def scatter_part(pieces, order):
    def wide(value):
        return value.astype(F32)

    first = order[0]
    kept = []
    for other in range(2):
        keep = (0, other) if first == "x" else (other, 0)
        send = (1, other) if first == "x" else (other, 1)
        moved = (swap_x if first == "x" else swap_y)(pieces[send])
        kept.append(wide(pieces[keep]) + wide(moved))
    swap = swap_y if first == "x" else swap_x
    if order[1] == "z":
        total = jnp.stack([kept[0][0], kept[1][0]])
        for k in (1, 2, 3):
            total = total + wide(swap_z(jnp.stack([kept[0][k], kept[1][k]]).astype(BF), k))
        return total[0] + wide(swap(total[1].astype(BF)))
    total = kept[0] + wide(swap(kept[1].astype(BF)))
    result = total[0]
    for k in (1, 2, 3):
        result = result + wide(swap_z(total[k].astype(BF), k))
    return result


def scatter_buffer(outs, orders):
    sums = []
    for index, order in enumerate(orders):
        pieces = {(i // 2, i % 2): outs[4 * index + i] for i in range(4)}
        sums.append(scatter_part(pieces, order))
    return jnp.concatenate(sums, axis=1)


def first_norm_kernel(pos, tokens, vectors, x_out, u_out):
    value = tokens[...]
    x_out[...] = value
    normed, _ = normalize(value)
    u_out[...] = (normed * (1.0 + vectors[1:2][None]) + vectors[0:1][None]).astype(BF)


def first_norm(pos, tokens, vectors):
    frames, places, width = tokens.shape
    step = places // 8
    return pl.pallas_call(
        first_norm_kernel,
        grid_spec=pltpu.PrefetchScalarGridSpec(
            num_scalar_prefetch=1,
            grid=(8,),
            in_specs=[
                pl.BlockSpec((2, step, width), lambda r, p: (p[2], p[3] ^ r, 0)),
                pl.BlockSpec((8, width), lambda r, p: (0, 0)),
            ],
            out_specs=[
                pl.BlockSpec((2, step, width), lambda r, p: (0, r, 0)),
                pl.BlockSpec((2, step, width), lambda r, p: (0, r, 0)),
            ],
        ),
        out_shape=[shape_of((2, places, width), F32), shape_of((2, places, width), BF)],
        compiler_params=params(),
        cost_estimate=cost(HALF * width * 12, HALF * width * 10),
    )(pos, tokens, vectors)


def later_norm_kernel(*refs):
    pieces, vectors, x_out, u_out = refs[:8], refs[8], refs[9], refs[10]
    for r in range(8):
        value = pieces[r][...].reshape(x_out.shape[0] // 8, -1)
        rows = pl.ds(r * value.shape[0], value.shape[0])
        x_out[rows, :] = value
        normed, _ = normalize(value.astype(F32))
        u_out[rows, :] = (normed * (1.0 + vectors[1:2]) + vectors[0:1]).astype(BF)


def later_norm(pieces, vectors):
    width = vectors.shape[1]
    return pl.pallas_call(
        later_norm_kernel,
        out_shape=[shape_of((HALF, width), BF), shape_of((HALF, width), BF)],
        compiler_params=pltpu.CompilerParams(vmem_limit_bytes=VMEM_LIMIT),
        cost_estimate=cost(HALF * width * 12, HALF * width * 6),
    )(*pieces, vectors)


def row_spec(width, rows=BLOCK):
    return pl.BlockSpec((rows, width), lambda b: (b, 0))


def whole_spec(*shape):
    return pl.BlockSpec(shape, lambda b: (0,) * len(shape))


def middle_kernel(x, a_own, a_other, vectors, x1_out, u_out):
    branch = a_own[...].astype(F32) + a_other[...].astype(F32)
    value = x[...].astype(F32) + vectors[2:3] * (branch + vectors[6:7])
    x1_out[...] = value
    normed, _ = normalize(value)
    u_out[...] = (normed * (1.0 + vectors[4:5]) + vectors[3:4]).astype(BF)


def middle_call(x, a_own, a_other, vectors):
    width = x.shape[1]
    return pl.pallas_call(
        middle_kernel,
        grid=(4,),
        in_specs=[row_spec(width, 128)] * 3 + [whole_spec(8, width)],
        out_specs=[row_spec(width, 128)] * 2,
        out_shape=[shape_of((HALF, width), F32), shape_of((HALF, width), BF)],
        compiler_params=params(),
        cost_estimate=cost(HALF * width * 16, HALF * width * 14),
    )(x, a_own, a_other, vectors)


def end_kernel(across, x1, m_own, m_other, vectors, *outs):
    branch = m_own[...].astype(F32) + m_other[...].astype(F32)
    value = (x1[...] + vectors[5:6] * (branch + vectors[7:8])).astype(BF)
    if across:
        for b in range(2):

            @pl.when(pl.program_id(0) == b)
            def _():
                outs[b][...] = value
    else:
        step = value.shape[0] // 8
        for r in range(8):
            outs[r][0] = value[r * step : (r + 1) * step]


def end_call(x1, m_own, m_other, vectors, across):
    width = x1.shape[1]
    if across:
        out_specs = [whole_spec(BLOCK, width)] * 2
        out_shape = [shape_of((BLOCK, width), BF)] * 2
    else:
        out_specs = [pl.BlockSpec((1, BLOCK // 8, width), lambda b: (b, 0, 0))] * 8
        out_shape = [shape_of((2, BLOCK // 8, width), BF)] * 8
    return pl.pallas_call(
        functools.partial(end_kernel, across),
        grid=(2,),
        in_specs=[row_spec(width)] * 3 + [whole_spec(8, width)],
        out_specs=out_specs,
        out_shape=out_shape,
        compiler_params=params(),
        cost_estimate=cost(HALF * width * 6, HALF * width * 10),
    )(x1, m_own, m_other, vectors)


def column_sum(value):
    return jnp.sum(value, axis=0, keepdims=True)


def add_rows(sums, rows):
    @pl.when(pl.program_id(0) == 0)
    def _():
        sums[...] = jnp.zeros_like(sums)

    for index, value in rows.items():
        sums[index : index + 1, :] += value


def before_kernel(across, *refs):
    count = 2 if across else 8
    pieces, (m_own, m_other, vectors, e_out, em_out, sums) = refs[:count], refs[count:]
    if across:
        grad = jnp.where(pl.program_id(0) == 0, pieces[0][...], pieces[1][...])
    else:
        grad = jnp.concatenate([p[0] for p in pieces], axis=0)
    e_out[...] = grad
    grad = grad.astype(F32)
    branch = m_own[...].astype(F32) + m_other[...].astype(F32)
    scaled = vectors[5:6] * grad
    em_out[...] = scaled.astype(BF)
    add_rows(sums, {5: column_sum(grad * (branch + vectors[7:8])), 7: column_sum(scaled)})


def before_call(pieces, m_own, m_other, vectors, across):
    width = vectors.shape[1]
    if across:
        specs = [whole_spec(BLOCK, width)] * 2
    else:
        specs = [pl.BlockSpec((1, BLOCK // 8, width), lambda b: (b, 0, 0))] * 8
    return pl.pallas_call(
        functools.partial(before_kernel, across),
        grid=(2,),
        in_specs=specs + [row_spec(width)] * 2 + [whole_spec(8, width)],
        out_specs=[row_spec(width)] * 2 + [whole_spec(8, width)],
        out_shape=[
            shape_of((HALF, width), BF),
            shape_of((HALF, width), BF),
            shape_of((8, width), F32),
        ],
        compiler_params=params(),
        cost_estimate=cost(HALF * width * 8, HALF * width * 10),
    )(*pieces, m_own, m_other, vectors)


def between_kernel(d_own, d_other, x1, e, a_own, a_other, vectors, e1_out, ea_out, sums):
    grad = d_own[...].astype(F32) + d_other[...].astype(F32)
    normed, inverse = normalize(x1[...])
    e1 = e[...].astype(F32) + norm_back(grad * (1.0 + vectors[4:5]), normed, inverse)
    e1_out[...] = e1
    branch = a_own[...].astype(F32) + a_other[...].astype(F32)
    scaled = vectors[2:3] * e1
    ea_out[...] = scaled.astype(BF)
    add_rows(
        sums,
        {
            3: column_sum(grad),
            4: column_sum(grad * normed),
            2: column_sum(e1 * (branch + vectors[6:7])),
            6: column_sum(scaled),
        },
    )


def between_call(d_own, d_other, x1, e, a_own, a_other, vectors):
    width = x1.shape[1]
    return pl.pallas_call(
        between_kernel,
        grid=(4,),
        in_specs=[row_spec(width, 128)] * 6 + [whole_spec(8, width)],
        out_specs=[row_spec(width, 128)] * 2 + [whole_spec(8, width)],
        out_shape=[
            shape_of((HALF, width), F32),
            shape_of((HALF, width), BF),
            shape_of((8, width), F32),
        ],
        compiler_params=params(),
        cost_estimate=cost(HALF * width * 30, HALF * width * 20),
    )(d_own, d_other, x1, e, a_own, a_other, vectors)


def after_kernel(across, d_own, d_other, x, e1, vectors, *outs):
    sums = outs[-1]
    grad = d_own[...].astype(F32) + d_other[...].astype(F32)
    normed, inverse = normalize(x[...].astype(F32))
    value = e1[...] + norm_back(grad * (1.0 + vectors[1:2]), normed, inverse)
    value = value.astype(BF)
    if across:
        step = value.shape[0] // 2
        for r in range(8):

            @pl.when(pl.program_id(0) == r // 2)
            def _():
                outs[r][...] = value[(r % 2) * step : (r % 2 + 1) * step].reshape(outs[r].shape)
    else:
        outs[0][...] = value
    add_rows(sums, {0: column_sum(grad), 1: column_sum(grad * normed)})


def after_call(d_own, d_other, x, e1, vectors, across):
    width = x.shape[1]
    if across:
        out_specs = [whole_spec(2, 32, width)] * 8
        out_shape = [shape_of((2, 32, width), BF)] * 8
    else:
        out_specs = [row_spec(width, 128)]
        out_shape = [shape_of((HALF, width), BF)]
    return pl.pallas_call(
        functools.partial(after_kernel, across),
        grid=(4,),
        in_specs=[row_spec(width, 128)] * 4 + [whole_spec(8, width)],
        out_specs=out_specs + [whole_spec(8, width)],
        out_shape=out_shape + [shape_of((8, width), F32)],
        compiler_params=params(),
        cost_estimate=cost(HALF * width * 24, HALF * width * 14),
    )(d_own, d_other, x, e1, vectors)


def viewed(across):
    return (16, 32) if across else (32, 16)


def half_spec(width, across, which):
    def index(b):
        at = jnp.minimum(b, 1) if which == 0 else jnp.maximum(b - 2, 0)
        return (0, at, 0) if across else (at, 0, 0)

    return pl.BlockSpec((16, 16, width), index)


def group_spec(width, across):
    def index(b):
        return (0, b // 2, 0, b % 2, 0) if across else (0, b // 2, b % 2, 0, 0)

    return pl.BlockSpec((2, 1, 16, 16, width), index)


def masked(scores):
    row = lax.broadcasted_iota(jnp.int32, scores.shape, 0)
    column = lax.broadcasted_iota(jnp.int32, scores.shape, 1)
    return (row - column) % 16 == 0


def attend_kernel(across, orders, pos, *refs):
    u_own, u_other, bias = refs[:3]
    weights, outs = refs[3:9], refs[9:14]
    qkv_out, o_out, lse_out, own_out, other_out = outs
    w_all, w_out, sems = refs[14:]
    b = pl.program_id(0)
    width = 3 * o_out.shape[-1]

    @pl.when(b == 0)
    def _():
        copies = weight_copies(
            weights, orders, (pos[0], pos[1]), w_all.shape[1] // 8, w_all, sems
        )
        for copy in copies:
            copy.start()
        for copy in copies:
            copy.wait()
        for g in range(2):
            w_out[g] = w_all[g, :, width:]

    u = jnp.where(b < 2, u_own[...], u_other[...]).reshape(BLOCK, -1)
    piece = width // 3
    total = None
    log_sums = []
    for g in range(2):
        joined = (nn(u, w_all[g, :, :width]) + bias[g]).astype(BF)
        qkv_out[g, 0] = joined.reshape(16, 16, width)
        found = []
        for n in range(piece // HEAD_DIM):
            at = n * HEAD_DIM
            query = joined[:, at : at + HEAD_DIM]
            keys = joined[:, piece + at : piece + at + HEAD_DIM]
            values = joined[:, 2 * piece + at : 2 * piece + at + HEAD_DIM]
            scores = nt(query, keys) * HEAD_DIM**-0.5
            if across:
                scores = jnp.where(masked(scores), scores, -1e30)
            top = jnp.max(scores, axis=-1, keepdims=True)
            expanded = jnp.exp(scores - top)
            sums = jnp.sum(expanded, axis=-1, keepdims=True)
            log_sums.append(top + jnp.log(sums))
            found.append(nn((expanded / sums).astype(BF), values))
        attended = jnp.concatenate(found, axis=1).astype(BF)
        o_out[g, 0] = attended.reshape(16, 16, piece)
        term = nt(attended, w_out[g])
        total = term if total is None else total + term
    lse_out[0, 0] = jnp.concatenate(log_sums, axis=1).reshape(16, 16, -1)
    total = total.astype(BF).reshape(16, 16, -1)

    @pl.when(b < 2)
    def _():
        own_out[...] = total

    @pl.when(b >= 2)
    def _():
        other_out[...] = total


def attend_call(pos, u_own, u_other, bias, weights, orders, across):
    width = u_own.shape[-1]
    wide = bias.shape[-1]
    piece = wide // 3
    lead = viewed(across)
    smem = pl.BlockSpec(memory_space=pltpu.SMEM)
    heads = 2 * piece // HEAD_DIM
    flops = 2 * 4 * BLOCK * width * 2 * 4 * piece + 4 * heads * 4 * BLOCK * BLOCK * 128
    lse_spec = pl.BlockSpec(
        (1, 1, 16, 16, heads),
        lambda b: (0, b // 2, 0, b % 2, 0) if across else (0, b // 2, b % 2, 0, 0),
    )
    return pl.pallas_call(
        functools.partial(attend_kernel, across, orders),
        grid=(4,),
        in_specs=[
            smem,
            half_spec(width, across, 0),
            half_spec(width, across, 1),
            whole_spec(2, 1, wide),
        ]
        + [ANY_SPEC] * 6,
        out_specs=[
            group_spec(wide, across),
            group_spec(piece, across),
            lse_spec,
            half_spec(width, across, 0),
            half_spec(width, across, 1),
        ],
        out_shape=[
            shape_of((2, 2) + lead + (wide,), BF),
            shape_of((2, 2) + lead + (piece,), BF),
            shape_of((1, 2) + lead + (heads,), F32),
            shape_of(lead + (width,), BF),
            shape_of(lead + (width,), BF),
        ],
        scratch_shapes=[
            pltpu.VMEM((2, width, wide + piece), BF),
            pltpu.VMEM((2, width, piece), BF),
            pltpu.SemaphoreType.DMA((64,)),
        ],
        compiler_params=params(),
        cost_estimate=cost(flops, 16 * 2**20, 4 * heads * BLOCK * BLOCK),
    )(pos, u_own.reshape(lead + (width,)), u_other.reshape(lead + (width,)), bias, *weights)


def attend_back_kernel(across, orders, pos, *refs):
    g_own, g_other, qkv, lse = refs[:4]
    weights, outs = refs[4:10], refs[10:14]
    dqkv_out, own_out, other_out, bias_out = outs
    w_all, w_out, sems = refs[14:]
    b = pl.program_id(0)
    width = qkv.shape[-1]

    @pl.when(b == 0)
    def _():
        copies = weight_copies(
            weights, orders, (pos[0], pos[1]), w_all.shape[1] // 8, w_all, sems
        )
        for copy in copies:
            copy.start()
        for copy in copies:
            copy.wait()
        for g in range(2):
            w_out[g] = w_all[g, :, width:]
        bias_out[...] = jnp.zeros_like(bias_out)

    grad = jnp.where(b < 2, g_own[...], g_other[...]).reshape(BLOCK, -1)
    piece = width // 3
    count = piece // HEAD_DIM
    log_sums = lse[0, 0].reshape(BLOCK, 2 * count)
    total = None
    for g in range(2):
        joined = qkv[g, 0].reshape(BLOCK, width)
        pulled = nn(grad, w_out[g]).astype(BF)
        found = [[], [], []]
        for n in range(count):
            at = n * HEAD_DIM
            query = joined[:, at : at + HEAD_DIM]
            keys = joined[:, piece + at : piece + at + HEAD_DIM]
            values = joined[:, 2 * piece + at : 2 * piece + at + HEAD_DIM]
            pull = pulled[:, at : at + HEAD_DIM]
            scores = nt(query, keys) * HEAD_DIM**-0.5
            if across:
                scores = jnp.where(masked(scores), scores, -1e30)
            probs = jnp.exp(scores - log_sums[:, g * count + n : g * count + n + 1])
            grad_probs = nt(pull, values)
            mean_term = jnp.sum(grad_probs * probs, axis=-1, keepdims=True)
            grad_scores = (probs * (grad_probs - mean_term)).astype(BF)
            found[0].append(nn(grad_scores, keys) * HEAD_DIM**-0.5)
            found[1].append(tn(grad_scores, query) * HEAD_DIM**-0.5)
            found[2].append(tn(probs.astype(BF), pull))
        triple = jnp.concatenate(found[0] + found[1] + found[2], axis=1).astype(BF)
        dqkv_out[g, 0] = triple.reshape(16, 16, width)
        bias_out[g] += column_sum(triple.astype(F32))
        term = nt(triple, w_all[g, :, :width])
        total = term if total is None else total + term
    total = total.astype(BF).reshape(16, 16, -1)

    @pl.when(b < 2)
    def _():
        own_out[...] = total

    @pl.when(b >= 2)
    def _():
        other_out[...] = total


def attend_back_call(pos, g_own, g_other, qkv, lse, weights, orders, across):
    width = g_own.shape[-1]
    wide = qkv.shape[-1]
    piece = wide // 3
    lead = viewed(across)
    smem = pl.BlockSpec(memory_space=pltpu.SMEM)
    heads = 2 * piece // HEAD_DIM
    flops = 2 * 4 * BLOCK * width * 2 * 4 * piece + 4 * heads * 10 * BLOCK * BLOCK * 128
    lse_spec = pl.BlockSpec(
        (1, 1, 16, 16, heads),
        lambda b: (0, b // 2, 0, b % 2, 0) if across else (0, b // 2, b % 2, 0, 0),
    )
    return pl.pallas_call(
        functools.partial(attend_back_kernel, across, orders),
        grid=(4,),
        in_specs=[
            smem,
            half_spec(width, across, 0),
            half_spec(width, across, 1),
            group_spec(wide, across),
            lse_spec,
        ]
        + [ANY_SPEC] * 6,
        out_specs=[
            group_spec(wide, across),
            half_spec(width, across, 0),
            half_spec(width, across, 1),
            whole_spec(2, 1, wide),
        ],
        out_shape=[
            shape_of((2, 2) + lead + (wide,), BF),
            shape_of(lead + (width,), BF),
            shape_of(lead + (width,), BF),
            shape_of((2, 1, wide), F32),
        ],
        scratch_shapes=[
            pltpu.VMEM((2, width, wide + piece), BF),
            pltpu.VMEM((2, width, piece), BF),
            pltpu.SemaphoreType.DMA((64,)),
        ],
        compiler_params=params(),
        cost_estimate=cost(flops, 20 * 2**20, 4 * heads * BLOCK * BLOCK),
    )(pos, g_own.reshape(lead + (width,)), g_other.reshape(lead + (width,)), qkv, lse, *weights)


def pick_spec(width, which):
    def index(b):
        return (jnp.minimum(b, 1) if which == 0 else jnp.maximum(b - 2, 0), 0)

    return pl.BlockSpec((BLOCK, width), index)


def hidden_spec(width):
    return pl.BlockSpec((2, BLOCK, width), lambda b: (0, b, 0))


def load_two(b, pos, up, down, orders_up, orders_down, w_up, w_down, sems):
    @pl.when(b == 0)
    def _():
        place = (pos[0], pos[1])
        rows = w_up.shape[1] // 8
        copies = weight_copies(up, orders_up, place, rows, w_up, sems.at[0])
        copies += weight_copies(down, orders_down, place, rows, w_down, sems.at[1])
        for copy in copies:
            copy.start()
        for copy in copies:
            copy.wait()


def expand_kernel(orders_up, orders_down, pos, *refs):
    u_own, u_other, bias = refs[:3]
    up, down, outs = refs[3:9], refs[9:15], refs[15:19]
    g_out, slope_out, own_out, other_out = outs
    w_up, w_down, sems = refs[19:]
    b = pl.program_id(0)
    load_two(b, pos, up, down, orders_up, orders_down, w_up, w_down, sems)
    u = jnp.where(b < 2, u_own[...], u_other[...])
    total = None
    for g in range(2):
        hidden = nn(u, w_up[g]) + bias[g]
        inner = 0.7978845608028654 * (hidden + 0.044715 * hidden * hidden * hidden)
        tangent = jnp.tanh(inner)
        active = (0.5 * hidden * (1.0 + tangent)).astype(BF)
        g_out[g] = active
        slope = 0.5 * (1.0 + tangent) + 0.5 * hidden * (1.0 - tangent * tangent) * (
            0.7978845608028654 * (1.0 + 3.0 * 0.044715 * hidden * hidden)
        )
        slope_out[g] = slope.astype(BF)
        term = nt(active, w_down[g])
        total = term if total is None else total + term
    total = total.astype(BF)

    @pl.when(b < 2)
    def _():
        own_out[...] = total

    @pl.when(b >= 2)
    def _():
        other_out[...] = total


def expand_call(pos, u_own, u_other, bias, up, down, orders_up, orders_down):
    width = u_own.shape[-1]
    units = bias.shape[-1]
    smem = pl.BlockSpec(memory_space=pltpu.SMEM)
    return pl.pallas_call(
        functools.partial(expand_kernel, orders_up, orders_down),
        grid=(4,),
        in_specs=[smem, pick_spec(width, 0), pick_spec(width, 1), whole_spec(2, 1, units)]
        + [ANY_SPEC] * 12,
        out_specs=[hidden_spec(units)] * 2 + [pick_spec(width, 0), pick_spec(width, 1)],
        out_shape=[
            shape_of((2, 2 * HALF, units), BF),
            shape_of((2, 2 * HALF, units), BF),
            shape_of((HALF, width), BF),
            shape_of((HALF, width), BF),
        ],
        scratch_shapes=[
            pltpu.VMEM((2, width, units), BF),
            pltpu.VMEM((2, width, units), BF),
            pltpu.SemaphoreType.DMA((2, 64)),
        ],
        compiler_params=params(),
        cost_estimate=cost(8 * 2 * HALF * width * units, 25 * 2**20, 4 * HALF * units),
    )(pos, u_own, u_other, bias, *up, *down)


def expand_back_kernel(orders_up, orders_down, pos, *refs):
    g_own, g_other, slope = refs[:3]
    up, down, outs = refs[3:9], refs[9:15], refs[15:19]
    dh_out, own_out, other_out, bias_out = outs
    w_up, w_down, sems = refs[19:]
    b = pl.program_id(0)
    load_two(b, pos, up, down, orders_up, orders_down, w_up, w_down, sems)

    @pl.when(b == 0)
    def _():
        bias_out[...] = jnp.zeros_like(bias_out)

    grad = jnp.where(b < 2, g_own[...], g_other[...])
    total = None
    for g in range(2):
        hidden = (nn(grad, w_down[g]) * slope[g].astype(F32)).astype(BF)
        dh_out[g] = hidden
        bias_out[g] += column_sum(hidden.astype(F32))
        term = nt(hidden, w_up[g])
        total = term if total is None else total + term
    total = total.astype(BF)

    @pl.when(b < 2)
    def _():
        own_out[...] = total

    @pl.when(b >= 2)
    def _():
        other_out[...] = total


def expand_back_call(pos, g_own, g_other, slope, up, down, orders_up, orders_down):
    width = g_own.shape[-1]
    units = slope.shape[-1]
    smem = pl.BlockSpec(memory_space=pltpu.SMEM)
    return pl.pallas_call(
        functools.partial(expand_back_kernel, orders_up, orders_down),
        grid=(4,),
        in_specs=[smem, pick_spec(width, 0), pick_spec(width, 1), hidden_spec(units)]
        + [ANY_SPEC] * 12,
        out_specs=[hidden_spec(units), pick_spec(width, 0), pick_spec(width, 1)]
        + [whole_spec(2, 1, units)],
        out_shape=[
            shape_of((2, 2 * HALF, units), BF),
            shape_of((HALF, width), BF),
            shape_of((HALF, width), BF),
            shape_of((2, 1, units), F32),
        ],
        scratch_shapes=[
            pltpu.VMEM((2, width, units), BF),
            pltpu.VMEM((2, width, units), BF),
            pltpu.SemaphoreType.DMA((2, 64)),
        ],
        compiler_params=params(),
        cost_estimate=cost(8 * 2 * HALF * width * units, 25 * 2**20),
    )(pos, g_own, g_other, slope, *up, *down)


def weight_grad_kernel(joint, pos, *refs):
    if joint:
        left, right, left_two, right_two = (refs[:2], refs[2], refs[3:5], refs[5])
        refs = refs[6:]
    else:
        left, right = refs[:2], refs[2]
        refs = refs[3:]
    outs, refs = refs[:12], refs[12:]
    stage, turned, sems = refs[0], refs[1], refs[-1]
    g, part = pl.program_id(0), pl.program_id(1)
    first = jnp.logical_and(g == 0, part == 0)
    last = jnp.logical_and(g == 1, part == 2)
    rows = turned.shape[0] // 8

    @pl.when(first)
    def _():
        for half in range(2):
            turned[:, half * HALF : (half + 1) * HALF] = left[half][...].T

    slot = g * 3 + part
    if joint:
        turned_two = refs[2]

        @pl.when(first)
        def _():
            for half in range(2):
                turned_two[:, half * HALF : (half + 1) * HALF] = left_two[half][...].T

        @pl.when(part < 2)
        def _():
            stage[slot] = nn(turned[...], right[0]).astype(BF)

        @pl.when(part == 2)
        def _():
            rest = PART - right_two.shape[-1]
            stage[slot] = jnp.concatenate(
                [nn(turned[...], right[0, :, :rest]), nn(turned_two[...], right_two[0])], axis=1
            ).astype(BF)
    else:
        stage[slot] = nn(turned[...], right[0]).astype(BF)

    def copies(group, index):
        made = []
        for y in range(2):
            for z in range(4):
                start = ((z ^ pos[0]) * 2 + (y ^ pos[1])) * rows
                made.append(
                    pltpu.make_async_copy(
                        stage.at[group * 3 + index, pl.ds(pl.multiple_of(start, 16), rows)],
                        outs[index * 4 + group * 2 + y].at[z],
                        sems.at[group * 3 + index, y * 4 + z],
                    )
                )
        return made

    for group in range(2):
        for index in range(3):

            @pl.when(jnp.logical_and(g == group, part == index))
            def _():
                for copy in copies(group, index):
                    copy.start()

    @pl.when(last)
    def _():
        for group in range(2):
            for index in range(3):
                for copy in copies(group, index):
                    copy.wait()


def weight_grad(pos, left, right, left_two=None, right_two=None):
    width = left[0].shape[-1]
    joint = left_two is not None
    smem = pl.BlockSpec(memory_space=pltpu.SMEM)

    def whole(*shape):
        return pl.BlockSpec(shape, lambda g, p: (0,) * len(shape))

    in_specs = [smem, whole(HALF, width), whole(HALF, width)]
    in_specs.append(pl.BlockSpec((1, 2 * HALF, PART), lambda g, p: (g, 0, p)))
    args = [pos, left[0], left[1], right]
    scratch = [pltpu.VMEM((6, width, PART), BF), pltpu.VMEM((width, 2 * HALF), BF)]
    if joint:
        in_specs += [whole(HALF, width), whole(HALF, width)]
        in_specs.append(
            pl.BlockSpec((1, 2 * HALF, right_two.shape[-1]), lambda g, p: (g, 0, 0))
        )
        args += [left_two[0], left_two[1], right_two]
        scratch.append(pltpu.VMEM((width, 2 * HALF), BF))
    return pl.pallas_call(
        functools.partial(weight_grad_kernel, joint),
        grid=(2, 3),
        in_specs=in_specs,
        out_specs=[ANY_SPEC] * 12,
        out_shape=[shape_of((4, width // 8, PART), BF)] * 12,
        scratch_shapes=scratch + [pltpu.SemaphoreType.DMA((6, 8))],
        compiler_params=params(2),
        cost_estimate=cost(2 * 2 * HALF * width * 6 * PART, 16 * 2**20),
    )(*args)


def spread_result_kernel(pos, *refs):
    pieces, out = refs[:8], refs[8]
    for source in range(4):
        for e in range(2):
            block = pos[3] ^ (4 * e + source)
            value = pieces[source * 2 + e][0]
            step = value.shape[1]
            out[:, pl.ds(pl.multiple_of(block * step, step), step), :] = value.astype(F32)


def spread_result(pos, pieces, places):
    _, pair, step, width = pieces[0].shape

    def spec(source):
        return pl.BlockSpec((1, pair, step, width), lambda t, p: (p[2] ^ source ^ t, 0, 0, 0))

    return pl.pallas_call(
        spread_result_kernel,
        grid_spec=pltpu.PrefetchScalarGridSpec(
            num_scalar_prefetch=1,
            grid=(4,),
            in_specs=[spec(source) for source in range(4) for _ in range(2)],
            out_specs=pl.BlockSpec((pair, places, width), lambda t, p: (t, 0, 0)),
        ),
        out_shape=shape_of((4 * pair, places, width), F32),
        compiler_params=params(),
        cost_estimate=cost(8 * HALF * width, 24 * HALF * width),
    )(pos, *pieces)


def spread_tokens_kernel(pos, *refs):
    pieces, out = refs[:4], refs[4]
    for source in range(4):

        @pl.when(pl.program_id(0) == source)
        def _():
            for r in range(8):
                block = pos[3] ^ source ^ r
                step = pieces[source].shape[2]
                out[:, pl.ds(pl.multiple_of(block * step, step), step), :] = pieces[source][
                    :, r
                ].astype(F32)


def spread_tokens(pos, pieces):
    pair, count, step, width = pieces[0].shape
    return pl.pallas_call(
        spread_tokens_kernel,
        grid_spec=pltpu.PrefetchScalarGridSpec(
            num_scalar_prefetch=1,
            grid=(4,),
            in_specs=[pl.BlockSpec((pair, count, step, width), lambda s, p: (0, 0, 0, 0))] * 4,
            out_specs=pl.BlockSpec(
                (pair, count * step, width), lambda s, p: (p[2] ^ s, 0, 0)
            ),
        ),
        out_shape=shape_of((4 * pair, count * step, width), F32),
        compiler_params=params(),
        cost_estimate=cost(8 * HALF * width, 24 * HALF * width),
    )(pos, *pieces)


def take_grad_kernel(pos, own, other, own_out, other_out):
    own_out[0] = own[...].astype(BF)
    other_out[0] = other[...].astype(BF)


def take_grad(pos, out_grad):
    _, places, width = out_grad.shape
    step = places // 8
    return pl.pallas_call(
        take_grad_kernel,
        grid_spec=pltpu.PrefetchScalarGridSpec(
            num_scalar_prefetch=1,
            grid=(4,),
            in_specs=[
                pl.BlockSpec((2, step, width), lambda j, p: (p[2] ^ j, p[3], 0)),
                pl.BlockSpec((2, step, width), lambda j, p: (p[2] ^ j, p[3] ^ 4, 0)),
            ],
            out_specs=[pl.BlockSpec((1, 2, step, width), lambda j, p: (j, 0, 0, 0))] * 2,
        ),
        out_shape=[shape_of((4, 2, step, width), BF)] * 2,
        compiler_params=params(),
        cost_estimate=cost(HALF * width, 6 * HALF * width),
    )(pos, out_grad, out_grad)


def pick(array, index):
    return lax.dynamic_index_in_dim(array, index, 0, keepdims=False)


def fast_body(
    tokens, condition, w_qkv, b_qv, w_out, b_out, w_up, b_up, w_down, b_down, w_mod, b_mod, out_grad
):
    z, y, hd = lax.axis_index("clip"), lax.axis_index("frame"), lax.axis_index("head")
    idx = 4 * y + hd
    pos = jnp.stack([z, y, hd, idx]).astype(jnp.int32)
    layers = w_qkv.shape[0]
    rows, piece, units = w_qkv.shape[1], w_qkv.shape[3], w_up.shape[2]
    width = tokens.shape[3]

    activated = jax.nn.silu(condition)
    partial = jnp.einsum("cd,ldje->clje", activated, w_mod, precision=highest)
    mine = pick(partial, z)
    for k in (1, 2, 3):
        mine = mine + swap_z(pick(partial, z ^ k), k)
    mine = mine + swap_y(mine)
    pair = jnp.stack([mine, swap_core(mine)])
    quarters = jnp.concatenate([pair, swap_x(pair)])
    mod = jnp.concatenate([pick(quarters, hd ^ q) for q in range(4)], axis=-1) + b_mod
    vectors = jnp.concatenate([mod, b_out[:, None], b_down[:, None]], axis=1)

    bias_rows = jnp.concatenate([b_qv.reshape(layers, -1), b_up], axis=1)
    bias_rows = jnp.stack([bias_rows, swap_x(bias_rows)])
    zeros = jnp.zeros((2, layers, piece), F32)
    bias_qkv = jnp.concatenate(
        [bias_rows[:, :, :piece], zeros, bias_rows[:, :, piece : 2 * piece]], axis=2
    )[:, :, None]
    bias_up = bias_rows[:, :, None, 2 * piece :]

    buffers, orders = [], []
    for l in range(layers):
        low = [
            jnp.concatenate([w_qkv[l].reshape(rows, 3 * piece), w_out[l].T], axis=1).astype(BF),
            w_up[l].astype(BF),
            w_down[l].T.astype(BF),
        ]
        for shard in low:
            orders.append(GATHER_ORDERS[len(orders) % 2])
            buffers.append(gather_buffer(shard, orders[-1]))

    grad_own, grad_send = take_grad(pos, out_grad[0])
    grad_other = swap_y(grad_send)

    saved = []
    pieces = None
    for l in range(layers):
        across = l == 1
        b_attn, b_up_w, b_down_w = buffers[3 * l : 3 * l + 3]
        o_attn, o_up, o_down = orders[3 * l : 3 * l + 3]
        if l == 0:
            x, u = first_norm(pos, tokens[0], vectors[0])
            x, u = x.reshape(HALF, width), u.reshape(HALF, width)
        else:
            x, u = later_norm(pieces, vectors[l])
        u_other = swap_core(u)
        qkv, o, lse, a_own, a_send = attend_call(
            pos, u, u_other, bias_qkv[:, l], b_attn, o_attn, across
        )
        a_own = a_own.reshape(HALF, width)
        a_other = swap_core(a_send.reshape(HALF, width))
        x1, u2 = middle_call(x, a_own, a_other, vectors[l])
        u2_other = swap_core(u2)
        active, slope, m_own, m_send = expand_call(
            pos, u2, u2_other, bias_up[:, l], b_up_w, b_down_w, o_up, o_down
        )
        m_other = swap_core(m_send)
        ended = end_call(x1, m_own, m_other, vectors[l], across)
        if not across:
            pieces = [ended[0]] + [swap_clip(ended[r], r) for r in range(1, 8)]
        saved.append(
            (x, u, u_other, qkv, o, lse, a_own, a_other, x1, u2, u2_other, active, slope)
            + (m_own, m_other)
        )

    halves = [value.reshape(4, 2, 32, width) for value in ended]
    pair = [halves[0], swap_y(halves[1])]
    pair_x = [swap_x(value) for value in pair]
    sources = [pair, [swap_core(v) for v in pair], pair_x, [swap_core(v) for v in pair_x]]
    result = spread_result(pos, [v for s in sources for v in s], tokens.shape[2])

    grads = [grad_own.reshape(BLOCK, width), grad_other.reshape(BLOCK, width)]
    sums, bias_sums, shards = [None] * layers, [None] * layers, [None] * layers
    for l in reversed(range(layers)):
        across = l == 1
        b_attn, b_up_w, b_down_w = buffers[3 * l : 3 * l + 3]
        o_attn, o_up, o_down = orders[3 * l : 3 * l + 3]
        (x, u, u_other, qkv, o, lse, a_own, a_other, x1, u2, u2_other, active, slope) = saved[l][
            :13
        ]
        m_own, m_other = saved[l][13:]
        e, em, sums_one = before_call(grads, m_own, m_other, vectors[l], across)
        em_other = swap_core(em)
        d_down = weight_grad(pos, (em, em_other), active)
        dh, d_own, d_send, up_sum = expand_back_call(
            pos, em, em_other, slope, b_up_w, b_down_w, o_up, o_down
        )
        d_other = swap_core(d_send)
        d_up = weight_grad(pos, (u2, u2_other), dh)
        e1, ea, sums_two = between_call(d_own, d_other, x1, e, a_own, a_other, vectors[l])
        ea_other = swap_core(ea)
        dqkv, d_own, d_send, qkv_sum = attend_back_call(
            pos, ea, ea_other, qkv, lse, b_attn, o_attn, across
        )
        d_other = swap_core(d_send.reshape(HALF, width))
        d_attn = weight_grad(
            pos,
            (u, u_other),
            dqkv.reshape(2, 2 * HALF, 3 * piece),
            (ea, ea_other),
            o.reshape(2, 2 * HALF, piece),
        )
        *ended, sums_three = after_call(
            d_own.reshape(HALF, width), d_other, x, e1, vectors[l], across
        )
        if across:
            grads = [ended[0]] + [swap_clip(ended[r], r) for r in range(1, 8)]
        sums[l] = sums_one + sums_two + sums_three
        bias_sums[l] = jnp.concatenate(
            [qkv_sum[:, 0, :piece], qkv_sum[:, 0, 2 * piece :], up_sum[:, 0]], axis=1
        )
        shards[l] = [
            scatter_buffer(outs, SCATTER_ORDERS[(3 * l + i) % 2])
            for i, outs in enumerate((d_attn, d_up, d_down))
        ]

    own = ended[0].reshape(2, 8, 32, width)
    own_x = swap_x(own)
    tokens_grad = spread_tokens(pos, [own, swap_core(own), own_x, swap_core(own_x)])

    clip_sums = jnp.stack(sums)
    kept = jnp.stack([b[0] for b in bias_sums])
    sent = jnp.stack([b[1] for b in bias_sums])
    count = clip_sums.size

    def flat(*values):
        return jnp.concatenate([v.reshape(-1) for v in values])

    total = flat(clip_sums, kept) + swap_x(flat(clip_sums, sent))
    total = total + swap_y(total)
    clip_part = total[:count].reshape(clip_sums.shape)
    clip_part = clip_part + swap_core(clip_part)
    total = flat(clip_part, total[count:])
    clips = [total] + [swap_z(total, k) for k in (1, 2, 3)]
    bias_total = sum(c[count:] for c in clips).reshape(kept.shape)
    by_clip = jnp.stack([c[:count].reshape(clip_sums.shape) for c in clips])
    all_clips = jnp.sum(by_clip, axis=0)
    b_mod_grad = all_clips[:, :6]
    b_out_grad, b_down_grad = all_clips[:, 6], all_clips[:, 7]
    b_qv_grad = bias_total[:, : 2 * piece].reshape(layers, 2, piece)
    b_up_grad = bias_total[:, 2 * piece :]

    columns = lax.dynamic_slice_in_dim(by_clip[:, :, :6], hd * piece, piece, 3)
    near = jnp.stack([pick(activated, z ^ k) for k in range(4)])
    w_mod_grad = sum(
        near[k][None, :, None, None] * columns[k][:, None] for k in range(4)
    )
    cond_part = jnp.einsum("clje,ldje->cd", columns, w_mod, precision=highest)
    cond_part = jnp.stack([pick(cond_part, z ^ k) for k in range(4)])
    cond_part = cond_part + swap_x(cond_part)
    cond_part = cond_part + swap_core(cond_part)
    sigma = jax.nn.sigmoid(condition)
    cond_grad = cond_part * sigma * (1.0 + condition * (1.0 - sigma))

    w_qkv_grad = jnp.stack(
        [s[0][:, : 3 * piece].reshape(rows, 3, piece) for s in shards]
    )
    w_out_grad = jnp.stack([s[0][:, 3 * piece :].T for s in shards])
    w_up_grad = jnp.stack([s[1] for s in shards])
    w_down_grad = jnp.stack([s[2].T for s in shards])
    return (
        result[None],
        tokens_grad[None],
        cond_grad,
        w_qkv_grad,
        b_qv_grad,
        w_out_grad,
        b_out_grad,
        w_up_grad,
        b_up_grad,
        w_down_grad,
        b_down_grad,
        w_mod_grad,
        b_mod_grad,
    )


def solution(mesh):
    sizes = dict(mesh.shape)
    fits = (sizes["clip"], sizes["frame"], sizes["head"]) == (4, 2, 4)
    return jax.shard_map(
        fast_body if fits else body,
        mesh=mesh,
        in_specs=(
            P("clip", "frame", None, None),
            P(None, ("clip", "frame")),
            P(None, ("clip", "frame"), None, "head"),
            P(None, None, "head"),
            P(None, "head", ("clip", "frame")),
            P(),
            P(None, ("clip", "frame"), "head"),
            P(None, "head"),
            P(None, "head", ("clip", "frame")),
            P(),
            P(None, ("clip", "frame"), None, "head"),
            P(),
            P("clip", "frame", None, None),
        ),
        out_specs=(
            P("clip", "frame", None, None),
            P("clip", "frame", None, None),
            P(None, ("clip", "frame")),
            P(None, ("clip", "frame"), None, "head"),
            P(None, None, "head"),
            P(None, "head", ("clip", "frame")),
            P(),
            P(None, ("clip", "frame"), "head"),
            P(None, "head"),
            P(None, "head", ("clip", "frame")),
            P(),
            P(None, ("clip", "frame"), None, "head"),
            P(),
        ),
        check_vma=False,
    )
```

```python
import functools
import itertools

import jax
import jax.numpy as jnp
from jax import lax
from jax.experimental import pallas as pl
from jax.experimental.pallas import tpu as pltpu
from jax.sharding import PartitionSpec as P

HEAD_DIM = 72


highest = lax.Precision.HIGHEST


def normalize(value):
    center = value - jnp.mean(value, axis=-1, keepdims=True)
    inverse = lax.rsqrt(jnp.mean(center * center, axis=-1, keepdims=True) + 1e-06)
    return (center * inverse, inverse)


def norm_back(grad, normed, inverse):
    first_mean = jnp.mean(grad, axis=-1, keepdims=True)
    second_mean = jnp.mean(grad * normed, axis=-1, keepdims=True)
    return inverse * (grad - first_mean - normed * second_mean)


def gelu_tanh(value):
    inner = 0.7978845608028654 * (value + 0.044715 * value * value * value)
    return 0.5 * value * (1.0 + jnp.tanh(inner))


def gelu_slope(value):
    inner = 0.7978845608028654 * (value + 0.044715 * value * value * value)
    tangent = jnp.tanh(inner)
    return 0.5 * (1.0 + tangent) + 0.5 * value * (1.0 - tangent * tangent) * 0.7978845608028654 * (
        1.0 + 3.0 * 0.044715 * value * value
    )


def score_specs(across):
    if across:
        return ("cabnk,cebnk->cbnae", "cbnae,cebnk->cabnk", "cbnae,cabnk->cebnk")
    return ("cabnk,caenk->canbe", "canbe,caenk->cabnk", "canbe,cabnk->caenk")


def branch_total(partial_value):
    share = lax.psum_scatter(
        partial_value.astype(jnp.bfloat16), "head", scatter_dimension=3, tiled=True
    ).astype(jnp.float32)
    return lax.all_gather(share.astype(jnp.bfloat16), "head", axis=3, tiled=True).astype(
        share.dtype
    )


def head_total(partial_value):
    share = lax.psum_scatter(
        partial_value.astype(jnp.bfloat16), "head", scatter_dimension=3, tiled=True
    ).astype(jnp.float32)
    return lax.all_gather(share.astype(jnp.bfloat16), "head", axis=3, tiled=True).astype(
        share.dtype
    )


def layer_forward(inputs, shifts, weights, biases, across):
    w_query, w_project, w_expand, w_reduce = weights
    bias_qv, bias_out, bias_up, bias_down = biases
    shape = inputs.shape
    width = w_query.shape[2]
    heads = width // HEAD_DIM
    first, second, third = score_specs(across)
    normed_one, inverse_one = normalize(inputs)
    mixed_one = (normed_one * (1.0 + shifts[1]) + shifts[0]).astype(jnp.bfloat16)
    joined = jnp.einsum("cabd,dje->cabje", mixed_one, w_query, preferred_element_type=jnp.float32)
    bias_full = jnp.stack([bias_qv[0], jnp.zeros_like(bias_qv[0]), bias_qv[1]])
    triple = (joined + bias_full).astype(jnp.bfloat16).reshape(shape[:3] + (3, heads, HEAD_DIM))
    query = triple[:, :, :, 0]
    keys = triple[:, :, :, 1]
    values = triple[:, :, :, 2]
    scores = jnp.einsum(first, query, keys, preferred_element_type=jnp.float32) * HEAD_DIM ** (-0.5)
    highest_score = jnp.max(scores, axis=-1, keepdims=True)
    expanded = jnp.exp(scores - highest_score)
    total = jnp.sum(expanded, axis=-1, keepdims=True)
    log_total = highest_score + jnp.log(total)
    soft_low = (expanded / total).astype(jnp.bfloat16)
    attended = jnp.einsum(second, soft_low, values, preferred_element_type=jnp.float32)
    attended = attended.astype(jnp.bfloat16).reshape(shape[:3] + (width,))
    partial_value = jnp.einsum(
        "cabe,ed->cabd", attended, w_project, preferred_element_type=jnp.float32
    )
    branch_one = branch_total(partial_value)
    middle = inputs + shifts[2] * (branch_one + bias_out)
    normed_two, inverse_two = normalize(middle)
    mixed_two = (normed_two * (1.0 + shifts[4]) + shifts[3]).astype(jnp.bfloat16)
    hidden = (
        jnp.einsum("cabd,df->cabf", mixed_two, w_expand, preferred_element_type=jnp.float32)
        + bias_up
    )
    activated = gelu_tanh(hidden).astype(jnp.bfloat16)
    partial_two = jnp.einsum(
        "cabf,fd->cabd", activated, w_reduce, preferred_element_type=jnp.float32
    )
    branch_two = branch_total(partial_two)
    output = middle + shifts[5] * (branch_two + bias_down)
    saved = (
        normed_one,
        inverse_one,
        mixed_one,
        query,
        keys,
        values,
        log_total,
        attended,
        branch_one,
        normed_two,
        inverse_two,
        mixed_two,
        hidden,
        activated,
        branch_two,
    )
    return (output, saved)


def layer_backward(grad_out, saved, shifts, weights, biases, across):
    (
        normed_one,
        inverse_one,
        mixed_one,
        query,
        keys,
        values,
        log_total,
        attended,
        branch_one,
        normed_two,
        inverse_two,
        mixed_two,
        hidden,
        activated,
        branch_two,
    ) = saved
    w_query, w_project, w_expand, w_reduce = weights
    bias_qv, bias_out, bias_up, bias_down = biases
    shape = grad_out.shape
    width = w_query.shape[2]
    first, second, third = score_specs(across)
    token_axes = (1, 2)
    every_axis = (0, 1, 2)
    dgate_two = jnp.sum(grad_out * (branch_two + bias_down), axis=token_axes)
    scaled_two = shifts[5] * grad_out
    grad_bias_down = jnp.sum(scaled_two, axis=every_axis)
    scaled_two_low = scaled_two.astype(jnp.bfloat16)
    grad_reduce = jnp.einsum(
        "cabf,cabd->fd", activated, scaled_two_low, preferred_element_type=jnp.float32
    )
    grad_active = jnp.einsum(
        "cabd,fd->cabf", scaled_two_low, w_reduce, preferred_element_type=jnp.float32
    )
    grad_hidden = (grad_active * gelu_slope(hidden)).astype(jnp.bfloat16)
    grad_bias_up = jnp.sum(grad_hidden, axis=every_axis, dtype=jnp.float32)
    grad_expand = jnp.einsum(
        "cabd,cabf->df", mixed_two, grad_hidden, preferred_element_type=jnp.float32
    )
    grad_mixed_two = head_total(
        jnp.einsum("cabf,df->cabd", grad_hidden, w_expand, preferred_element_type=jnp.float32)
    )
    dshift_two = jnp.sum(grad_mixed_two, axis=token_axes)
    dscale_two = jnp.sum(grad_mixed_two * normed_two, axis=token_axes)
    grad_middle = grad_out + norm_back(grad_mixed_two * (1.0 + shifts[4]), normed_two, inverse_two)
    dgate_one = jnp.sum(grad_middle * (branch_one + bias_out), axis=token_axes)
    scaled_one = shifts[2] * grad_middle
    grad_bias_out = jnp.sum(scaled_one, axis=every_axis)
    scaled_one_low = scaled_one.astype(jnp.bfloat16)
    grad_project = jnp.einsum(
        "cabe,cabd->ed", attended, scaled_one_low, preferred_element_type=jnp.float32
    )
    grad_attended = jnp.einsum(
        "cabd,ed->cabe", scaled_one_low, w_project, preferred_element_type=jnp.float32
    )
    grad_attended = grad_attended.astype(jnp.bfloat16).reshape(query.shape)
    scores = jnp.einsum(first, query, keys, preferred_element_type=jnp.float32) * HEAD_DIM ** (-0.5)
    probs = jnp.exp(scores - log_total)
    grad_probs = jnp.einsum(first, grad_attended, values, preferred_element_type=jnp.float32)
    grad_values = jnp.einsum(
        third, probs.astype(jnp.bfloat16), grad_attended, preferred_element_type=jnp.float32
    )
    mean_term = jnp.sum(grad_probs * probs, axis=-1, keepdims=True)
    grad_scores = (probs * (grad_probs - mean_term)).astype(jnp.bfloat16)
    grad_query = jnp.einsum(
        second, grad_scores, keys, preferred_element_type=jnp.float32
    ) * HEAD_DIM ** (-0.5)
    grad_keys = jnp.einsum(
        third, grad_scores, query, preferred_element_type=jnp.float32
    ) * HEAD_DIM ** (-0.5)
    grad_triple = jnp.stack([grad_query, grad_keys, grad_values], axis=3).astype(jnp.bfloat16)
    grad_triple = grad_triple.reshape(shape[:3] + (3, width))
    grad_bias_qv = jnp.sum(grad_triple[:, :, :, 0::2], axis=every_axis, dtype=jnp.float32)
    grad_query_weight = jnp.einsum(
        "cabd,cabje->dje", mixed_one, grad_triple, preferred_element_type=jnp.float32
    )
    grad_mixed_one = head_total(
        jnp.einsum("cabje,dje->cabd", grad_triple, w_query, preferred_element_type=jnp.float32)
    )
    dshift_one = jnp.sum(grad_mixed_one, axis=token_axes)
    dscale_one = jnp.sum(grad_mixed_one * normed_one, axis=token_axes)
    grad_inputs = grad_middle + norm_back(
        grad_mixed_one * (1.0 + shifts[1]), normed_one, inverse_one
    )
    grad_shifts = jnp.stack(
        [dshift_one, dscale_one, dgate_one, dshift_two, dscale_two, dgate_two], axis=1
    )
    weight_grads = (grad_query_weight, grad_project, grad_expand, grad_reduce)
    bias_grads = (grad_bias_qv, grad_bias_out, grad_bias_up, grad_bias_down)
    return (grad_inputs, grad_shifts, weight_grads, bias_grads)


def body(
    tokens, condition, w_qkv, b_qv, w_out, b_out, w_up, b_up, w_down, b_down, w_mod, b_mod, out_grad
):
    clip_count = tokens.shape[0]
    columns = w_mod.shape[3]
    head_start = lax.axis_index("head") * columns
    clip_start = lax.axis_index("clip") * clip_count
    activated_cond = jax.nn.silu(condition)
    partial_value = jnp.einsum("cd,ldje->lcje", activated_cond, w_mod, precision=highest)
    spread = jnp.zeros(partial_value.shape[:3] + (columns * lax.axis_size("head"),), jnp.float32)
    spread = lax.dynamic_update_slice_in_dim(spread, partial_value, head_start, 3)
    modulation = lax.psum(spread, ("clip", "frame", "head")) + b_mod[:, None]
    own = lax.dynamic_slice_in_dim(modulation, clip_start, clip_count, 1)
    factors = own[:, :, :, None, None, :]
    shifts_first = [factors[0, :, index] for index in range(6)]
    shifts_second = [factors[1, :, index] for index in range(6)]
    biases_first = (b_qv[0], b_out[0], b_up[0], b_down[0])
    biases_second = (b_qv[1], b_out[1], b_up[1], b_down[1])

    def gather_copies(layer_index):
        return (
            lax.all_gather(
                w_qkv[layer_index].astype(jnp.bfloat16), ("clip", "frame"), axis=0, tiled=True
            ),
            lax.all_gather(
                w_out[layer_index].astype(jnp.bfloat16), ("clip", "frame"), axis=1, tiled=True
            ),
            lax.all_gather(
                w_up[layer_index].astype(jnp.bfloat16), ("clip", "frame"), axis=0, tiled=True
            ),
            lax.all_gather(
                w_down[layer_index].astype(jnp.bfloat16), ("clip", "frame"), axis=1, tiled=True
            ),
        )

    def regather(layer_index):
        return (
            lax.all_gather(
                w_qkv[layer_index].astype(jnp.bfloat16), ("clip", "frame"), axis=0, tiled=True
            ),
            lax.all_gather(
                w_out[layer_index].astype(jnp.bfloat16), ("clip", "frame"), axis=1, tiled=True
            ),
            lax.all_gather(
                w_up[layer_index].astype(jnp.bfloat16), ("clip", "frame"), axis=0, tiled=True
            ),
            lax.all_gather(
                w_down[layer_index].astype(jnp.bfloat16), ("clip", "frame"), axis=1, tiled=True
            ),
        )

    def return_grads(grads):
        return (
            lax.psum_scatter(grads[0], ("clip", "frame"), scatter_dimension=0, tiled=True),
            lax.psum_scatter(grads[1], ("clip", "frame"), scatter_dimension=1, tiled=True),
            lax.psum_scatter(grads[2], ("clip", "frame"), scatter_dimension=0, tiled=True),
            lax.psum_scatter(grads[3], ("clip", "frame"), scatter_dimension=1, tiled=True),
        )

    first_weights = gather_copies(0)
    middle, first_saved = layer_forward(tokens, shifts_first, first_weights, biases_first, False)
    placed = lax.all_to_all(
        middle.astype(jnp.bfloat16), "frame", split_axis=2, concat_axis=1, tiled=True
    ).astype(middle.dtype)
    second_weights = gather_copies(1)
    final, second_saved = layer_forward(placed, shifts_second, second_weights, biases_second, True)
    result = lax.all_to_all(
        final.astype(jnp.bfloat16), "frame", split_axis=1, concat_axis=2, tiled=True
    ).astype(final.dtype)
    second_weights = regather(1)
    grad_placed = lax.all_to_all(
        out_grad.astype(jnp.bfloat16), "frame", split_axis=2, concat_axis=1, tiled=True
    ).astype(out_grad.dtype)
    grad_second, mod_second, wgrad_second, bgrad_second = layer_backward(
        grad_placed, second_saved, shifts_second, second_weights, biases_second, True
    )
    shard_second = return_grads(wgrad_second)
    grad_middle = lax.all_to_all(
        grad_second.astype(jnp.bfloat16), "frame", split_axis=1, concat_axis=2, tiled=True
    ).astype(grad_second.dtype)
    first_weights = regather(0)
    tokens_grad, mod_first, wgrad_first, bgrad_first = layer_backward(
        grad_middle, first_saved, shifts_first, first_weights, biases_first, False
    )
    shard_first = return_grads(wgrad_first)
    stacked_mod = jnp.stack([mod_first, mod_second])
    placed_mod = lax.dynamic_update_slice_in_dim(
        jnp.zeros_like(modulation), stacked_mod, clip_start, 1
    )
    total_mod, total_qv, total_out, total_up, total_down = lax.psum(
        (
            placed_mod,
            jnp.stack([bgrad_first[0], bgrad_second[0]]),
            jnp.stack([bgrad_first[1], bgrad_second[1]]),
            jnp.stack([bgrad_first[2], bgrad_second[2]]),
            jnp.stack([bgrad_first[3], bgrad_second[3]]),
        ),
        ("clip", "frame"),
    )
    b_mod_grad = jnp.sum(total_mod, axis=1)
    mod_columns = lax.dynamic_slice_in_dim(total_mod, head_start, columns, 3)
    w_mod_grad = jnp.einsum("cd,lcje->ldje", activated_cond, mod_columns, precision=highest)
    cond_part = jnp.einsum("lcje,ldje->cd", mod_columns, w_mod, precision=highest)
    cond_total = lax.psum(cond_part, "head")
    sigma = jax.nn.sigmoid(condition)
    cond_grad = cond_total * sigma * (1.0 + condition * (1.0 - sigma))
    w_qkv_grad = jnp.stack([shard_first[0], shard_second[0]])
    w_out_grad = jnp.stack([shard_first[1], shard_second[1]])
    w_up_grad = jnp.stack([shard_first[2], shard_second[2]])
    w_down_grad = jnp.stack([shard_first[3], shard_second[3]])
    return (
        result,
        tokens_grad,
        cond_grad,
        w_qkv_grad,
        total_qv,
        w_out_grad,
        total_out,
        w_up_grad,
        total_up,
        w_down_grad,
        total_down,
        w_mod_grad,
        b_mod_grad,
    )


BF = jnp.bfloat16
F32 = jnp.float32
PART = 384
HALF = 512
BLOCK = 256
VMEM_LIMIT = 60 * 1024 * 1024
GATHERS = (
    ((0, 640, "baxy"), (640, 512, "bayx")),
    ((0, 1152, "bayx"),),
    ((0, 1152, "baxy"),),
    ((0, 1152, "bayx"),),
    ((0, 1152, "baxy"),),
    ((0, 1152, "bayx"),),
)
SCATTERS = ("xyab", "yxab", "xyab", "yxab", "xyab", "yxab")


def nn(a, b):
    return lax.dot_general(a, b, (((1,), (0,)), ((), ())), preferred_element_type=F32)


def nt(a, b):
    return lax.dot_general(a, b, (((1,), (1,)), ((), ())), preferred_element_type=F32)


def tn(a, b):
    return lax.dot_general(a, b, (((0,), (0,)), ((), ())), preferred_element_type=F32)


def xor_pairs(size, bit):
    return [(i, i ^ bit) for i in range(size)]


def swap_core(value):
    return lax.ppermute(value, "head", xor_pairs(4, 1))


def swap_x(value):
    return lax.ppermute(value, "head", xor_pairs(4, 2))


def swap_y(value):
    return lax.ppermute(value, "frame", xor_pairs(2, 1))


def swap_z(value, bit):
    return lax.ppermute(value, "clip", xor_pairs(4, bit))


def swap_clip(value, bit):
    return lax.ppermute(value, ("frame", "head"), xor_pairs(8, bit))


def params(steps=1, **extra):
    return pltpu.CompilerParams(
        dimension_semantics=("arbitrary",) * steps, vmem_limit_bytes=VMEM_LIMIT, **extra
    )


def cost(flops, moved, exps=0):
    return pl.CostEstimate(flops=int(flops), bytes_accessed=int(moved), transcendentals=int(exps))


def shape_of(shape, dtype):
    return jax.ShapeDtypeStruct(tuple(shape), dtype)


def swap_along(axis, value):
    if axis == "x":
        return swap_x(value)
    if axis == "y":
        return swap_y(value)
    return swap_z(value, 1 if axis == "a" else 2)


def gather_buffer(shard, parts):
    found = []
    for start, width, order in parts:
        current = shard[:, start : start + width]
        for axis in order[:3]:
            current = jnp.stack([current, swap_along(axis, current)])
        found += [current, swap_along(order[3], current)]
    return found


def weight_copies(refs, parts, place, rows, target, sems):
    z, y = place
    copies = []
    for index, (start, width, order) in enumerate(parts):
        for last, third, second, first in itertools.product(range(2), repeat=4):
            at = dict(zip(order, (first, second, third, last)))
            row = (((2 * at["b"] + at["a"]) ^ z) * 2 + (at["y"] ^ y)) * rows
            copies.append(
                pltpu.make_async_copy(
                    refs[2 * index + last].at[third, second, first],
                    target.at[
                        at["x"],
                        pl.ds(pl.multiple_of(row, 16), rows),
                        pl.ds(start, width),
                    ],
                    sems.at[len(copies)],
                )
            )
    return copies


ANY_SPEC = pl.BlockSpec(memory_space=pl.ANY)


def scatter_buffer(outs, order):
    keep, send = outs
    for axis in order[:3]:
        moved = swap_along(axis, send)
        send = (keep[1].astype(F32) + moved[1].astype(F32)).astype(BF)
        keep = (keep[0].astype(F32) + moved[0].astype(F32)).astype(BF)
    return keep.astype(F32) + swap_along(order[3], send).astype(F32)


def first_norm_kernel(pos, tokens, vectors, x_out, u_out):
    value = tokens[...]
    x_out[...] = value
    normed, _ = normalize(value)
    u_out[...] = (normed * (1.0 + vectors[1:2][None]) + vectors[0:1][None]).astype(BF)


def first_norm(pos, tokens, vectors):
    frames, places, width = tokens.shape
    step = places // 8
    return pl.pallas_call(
        first_norm_kernel,
        grid_spec=pltpu.PrefetchScalarGridSpec(
            num_scalar_prefetch=1,
            grid=(8,),
            in_specs=[
                pl.BlockSpec((2, step, width), lambda r, p: (p[2], p[3] ^ r, 0)),
                pl.BlockSpec((8, width), lambda r, p: (0, 0)),
            ],
            out_specs=[
                pl.BlockSpec((2, step, width), lambda r, p: (0, r, 0)),
                pl.BlockSpec((2, step, width), lambda r, p: (0, r, 0)),
            ],
        ),
        out_shape=[shape_of((2, places, width), F32), shape_of((2, places, width), BF)],
        compiler_params=params(),
        cost_estimate=cost(HALF * width * 12, HALF * width * 10),
    )(pos, tokens, vectors)


def later_norm_kernel(*refs):
    pieces, vectors, x_out, u_out = refs[:8], refs[8], refs[9], refs[10]
    for r in range(8):
        value = pieces[r][...].reshape(x_out.shape[0] // 8, -1)
        rows = pl.ds(r * value.shape[0], value.shape[0])
        x_out[rows, :] = value
        normed, _ = normalize(value.astype(F32))
        u_out[rows, :] = (normed * (1.0 + vectors[1:2]) + vectors[0:1]).astype(BF)


def later_norm(pieces, vectors):
    width = vectors.shape[1]
    return pl.pallas_call(
        later_norm_kernel,
        out_shape=[shape_of((HALF, width), BF), shape_of((HALF, width), BF)],
        compiler_params=pltpu.CompilerParams(vmem_limit_bytes=VMEM_LIMIT),
        cost_estimate=cost(HALF * width * 12, HALF * width * 6),
    )(*pieces, vectors)


def row_spec(width, rows=BLOCK):
    return pl.BlockSpec((rows, width), lambda b: (b, 0))


def whole_spec(*shape):
    return pl.BlockSpec(shape, lambda b: (0,) * len(shape))


def middle_kernel(x, a_own, a_other, vectors, x1_out, u_out):
    branch = a_own[...].astype(F32) + a_other[...].astype(F32)
    value = x[...].astype(F32) + vectors[2:3] * (branch + vectors[6:7])
    x1_out[...] = value
    normed, _ = normalize(value)
    u_out[...] = (normed * (1.0 + vectors[4:5]) + vectors[3:4]).astype(BF)


def middle_call(x, a_own, a_other, vectors):
    width = x.shape[1]
    return pl.pallas_call(
        middle_kernel,
        grid=(4,),
        in_specs=[row_spec(width, 128)] * 3 + [whole_spec(8, width)],
        out_specs=[row_spec(width, 128)] * 2,
        out_shape=[shape_of((HALF, width), F32), shape_of((HALF, width), BF)],
        compiler_params=params(),
        cost_estimate=cost(HALF * width * 16, HALF * width * 14),
    )(x, a_own, a_other, vectors)


def end_kernel(across, x1, m_own, m_other, vectors, *outs):
    branch = m_own[...].astype(F32) + m_other[...].astype(F32)
    value = (x1[...] + vectors[5:6] * (branch + vectors[7:8])).astype(BF)
    if across:
        for b in range(2):

            @pl.when(pl.program_id(0) == b)
            def _():
                outs[b][...] = value
    else:
        step = value.shape[0] // 8
        for r in range(8):
            outs[r][0] = value[r * step : (r + 1) * step]


def end_call(x1, m_own, m_other, vectors, across):
    width = x1.shape[1]
    if across:
        out_specs = [whole_spec(BLOCK, width)] * 2
        out_shape = [shape_of((BLOCK, width), BF)] * 2
    else:
        out_specs = [pl.BlockSpec((1, BLOCK // 8, width), lambda b: (b, 0, 0))] * 8
        out_shape = [shape_of((2, BLOCK // 8, width), BF)] * 8
    return pl.pallas_call(
        functools.partial(end_kernel, across),
        grid=(2,),
        in_specs=[row_spec(width)] * 3 + [whole_spec(8, width)],
        out_specs=out_specs,
        out_shape=out_shape,
        compiler_params=params(),
        cost_estimate=cost(HALF * width * 6, HALF * width * 10),
    )(x1, m_own, m_other, vectors)


def column_sum(value):
    return jnp.sum(value, axis=0, keepdims=True)


def add_rows(sums, rows):
    @pl.when(pl.program_id(0) == 0)
    def _():
        sums[...] = jnp.zeros_like(sums)

    for index, value in rows.items():
        sums[index : index + 1, :] += value


def before_kernel(across, *refs):
    count = 2 if across else 8
    pieces, (m_own, m_other, vectors, e_out, em_out, sums) = refs[:count], refs[count:]
    if across:
        grad = jnp.where(pl.program_id(0) == 0, pieces[0][...], pieces[1][...])
    else:
        grad = jnp.concatenate([p[0] for p in pieces], axis=0)
    e_out[...] = grad
    grad = grad.astype(F32)
    branch = m_own[...].astype(F32) + m_other[...].astype(F32)
    scaled = vectors[5:6] * grad
    em_out[...] = scaled.astype(BF)
    add_rows(sums, {5: column_sum(grad * (branch + vectors[7:8])), 7: column_sum(scaled)})


def before_call(pieces, m_own, m_other, vectors, across):
    width = vectors.shape[1]
    if across:
        specs = [whole_spec(BLOCK, width)] * 2
    else:
        specs = [pl.BlockSpec((1, BLOCK // 8, width), lambda b: (b, 0, 0))] * 8
    return pl.pallas_call(
        functools.partial(before_kernel, across),
        grid=(2,),
        in_specs=specs + [row_spec(width)] * 2 + [whole_spec(8, width)],
        out_specs=[row_spec(width)] * 2 + [whole_spec(8, width)],
        out_shape=[
            shape_of((HALF, width), BF),
            shape_of((HALF, width), BF),
            shape_of((8, width), F32),
        ],
        compiler_params=params(),
        cost_estimate=cost(HALF * width * 8, HALF * width * 10),
    )(*pieces, m_own, m_other, vectors)


def between_kernel(d_own, d_other, x1, e, a_own, a_other, vectors, e1_out, ea_out, sums):
    grad = d_own[...].astype(F32) + d_other[...].astype(F32)
    normed, inverse = normalize(x1[...])
    e1 = e[...].astype(F32) + norm_back(grad * (1.0 + vectors[4:5]), normed, inverse)
    e1_out[...] = e1
    branch = a_own[...].astype(F32) + a_other[...].astype(F32)
    scaled = vectors[2:3] * e1
    ea_out[...] = scaled.astype(BF)
    add_rows(
        sums,
        {
            3: column_sum(grad),
            4: column_sum(grad * normed),
            2: column_sum(e1 * (branch + vectors[6:7])),
            6: column_sum(scaled),
        },
    )


def between_call(d_own, d_other, x1, e, a_own, a_other, vectors):
    width = x1.shape[1]
    return pl.pallas_call(
        between_kernel,
        grid=(4,),
        in_specs=[row_spec(width, 128)] * 6 + [whole_spec(8, width)],
        out_specs=[row_spec(width, 128)] * 2 + [whole_spec(8, width)],
        out_shape=[
            shape_of((HALF, width), F32),
            shape_of((HALF, width), BF),
            shape_of((8, width), F32),
        ],
        compiler_params=params(),
        cost_estimate=cost(HALF * width * 30, HALF * width * 20),
    )(d_own, d_other, x1, e, a_own, a_other, vectors)


def after_kernel(across, d_own, d_other, x, e1, vectors, *outs):
    sums = outs[-1]
    grad = d_own[...].astype(F32) + d_other[...].astype(F32)
    normed, inverse = normalize(x[...].astype(F32))
    value = e1[...] + norm_back(grad * (1.0 + vectors[1:2]), normed, inverse)
    value = value.astype(BF)
    if across:
        step = value.shape[0] // 2
        for r in range(8):

            @pl.when(pl.program_id(0) == r // 2)
            def _():
                outs[r][...] = value[(r % 2) * step : (r % 2 + 1) * step].reshape(outs[r].shape)
    else:
        outs[0][...] = value
    add_rows(sums, {0: column_sum(grad), 1: column_sum(grad * normed)})


def after_call(d_own, d_other, x, e1, vectors, across):
    width = x.shape[1]
    if across:
        out_specs = [whole_spec(2, 32, width)] * 8
        out_shape = [shape_of((2, 32, width), BF)] * 8
    else:
        out_specs = [row_spec(width, 128)]
        out_shape = [shape_of((HALF, width), BF)]
    return pl.pallas_call(
        functools.partial(after_kernel, across),
        grid=(4,),
        in_specs=[row_spec(width, 128)] * 4 + [whole_spec(8, width)],
        out_specs=out_specs + [whole_spec(8, width)],
        out_shape=out_shape + [shape_of((8, width), F32)],
        compiler_params=params(),
        cost_estimate=cost(HALF * width * 24, HALF * width * 14),
    )(d_own, d_other, x, e1, vectors)


def viewed(across):
    return (16, 32) if across else (32, 16)


def half_spec(width, across, which):
    def index(b):
        at = jnp.minimum(b, 1) if which == 0 else jnp.maximum(b - 2, 0)
        return (0, at, 0) if across else (at, 0, 0)

    return pl.BlockSpec((16, 16, width), index)


def group_spec(width, across):
    def index(b):
        return (0, b // 2, 0, b % 2, 0) if across else (0, b // 2, b % 2, 0, 0)

    return pl.BlockSpec((2, 1, 16, 16, width), index)


def masked(scores):
    row = lax.broadcasted_iota(jnp.int32, scores.shape, 0)
    column = lax.broadcasted_iota(jnp.int32, scores.shape, 1)
    return (row - column) % 16 == 0


def attend_kernel(across, orders, pos, *refs):
    count = 2 * len(orders)
    u_own, u_other, bias = refs[:3]
    weights, outs = refs[3 : 3 + count], refs[3 + count : 8 + count]
    qkv_out, o_out, lse_out, own_out, other_out = outs
    w_all, w_out, sems = refs[8 + count :]
    b = pl.program_id(0)
    width = 3 * o_out.shape[-1]

    @pl.when(b == 0)
    def _():
        copies = weight_copies(
            weights, orders, (pos[0], pos[1]), w_all.shape[1] // 8, w_all, sems
        )
        for copy in copies:
            copy.start()
        for copy in copies:
            copy.wait()
        for g in range(2):
            w_out[g] = w_all[g, :, width:]

    u = jnp.where(b < 2, u_own[...], u_other[...]).reshape(BLOCK, -1)
    piece = width // 3
    total = None
    log_sums = []
    for g in range(2):
        joined = (nn(u, w_all[g, :, :width]) + bias[g]).astype(BF)
        qkv_out[g, 0] = joined.reshape(16, 16, width)
        found = []
        for n in range(piece // HEAD_DIM):
            at = n * HEAD_DIM
            query = joined[:, at : at + HEAD_DIM]
            keys = joined[:, piece + at : piece + at + HEAD_DIM]
            values = joined[:, 2 * piece + at : 2 * piece + at + HEAD_DIM]
            scores = nt(query, keys) * HEAD_DIM**-0.5
            if across:
                scores = jnp.where(masked(scores), scores, -1e30)
            top = jnp.max(scores, axis=-1, keepdims=True)
            expanded = jnp.exp(scores - top)
            sums = jnp.sum(expanded, axis=-1, keepdims=True)
            log_sums.append(top + jnp.log(sums))
            found.append(nn((expanded / sums).astype(BF), values))
        attended = jnp.concatenate(found, axis=1).astype(BF)
        o_out[g, 0] = attended.reshape(16, 16, piece)
        term = nt(attended, w_out[g])
        total = term if total is None else total + term
    lse_out[0, 0] = jnp.concatenate(log_sums, axis=1).reshape(16, 16, -1)
    total = total.astype(BF).reshape(16, 16, -1)

    @pl.when(b < 2)
    def _():
        own_out[...] = total

    @pl.when(b >= 2)
    def _():
        other_out[...] = total


def attend_call(pos, u_own, u_other, bias, weights, orders, across):
    width = u_own.shape[-1]
    wide = bias.shape[-1]
    piece = wide // 3
    lead = viewed(across)
    smem = pl.BlockSpec(memory_space=pltpu.SMEM)
    heads = 2 * piece // HEAD_DIM
    flops = 2 * 4 * BLOCK * width * 2 * 4 * piece + 4 * heads * 4 * BLOCK * BLOCK * 128
    lse_spec = pl.BlockSpec(
        (1, 1, 16, 16, heads),
        lambda b: (0, b // 2, 0, b % 2, 0) if across else (0, b // 2, b % 2, 0, 0),
    )
    return pl.pallas_call(
        functools.partial(attend_kernel, across, orders),
        grid=(4,),
        in_specs=[
            smem,
            half_spec(width, across, 0),
            half_spec(width, across, 1),
            whole_spec(2, 1, wide),
        ]
        + [ANY_SPEC] * len(weights),
        out_specs=[
            group_spec(wide, across),
            group_spec(piece, across),
            lse_spec,
            half_spec(width, across, 0),
            half_spec(width, across, 1),
        ],
        out_shape=[
            shape_of((2, 2) + lead + (wide,), BF),
            shape_of((2, 2) + lead + (piece,), BF),
            shape_of((1, 2) + lead + (heads,), F32),
            shape_of(lead + (width,), BF),
            shape_of(lead + (width,), BF),
        ],
        scratch_shapes=[
            pltpu.VMEM((2, width, wide + piece), BF),
            pltpu.VMEM((2, width, piece), BF),
            pltpu.SemaphoreType.DMA((64,)),
        ],
        compiler_params=params(),
        cost_estimate=cost(flops, 16 * 2**20, 4 * heads * BLOCK * BLOCK),
    )(pos, u_own.reshape(lead + (width,)), u_other.reshape(lead + (width,)), bias, *weights)


def attend_back_kernel(across, orders, pos, *refs):
    count = 2 * len(orders)
    g_own, g_other, qkv, lse = refs[:4]
    weights, outs = refs[4 : 4 + count], refs[4 + count : 8 + count]
    dqkv_out, own_out, other_out, bias_out = outs
    w_all, w_out, sems = refs[8 + count :]
    b = pl.program_id(0)
    width = qkv.shape[-1]

    @pl.when(b == 0)
    def _():
        copies = weight_copies(
            weights, orders, (pos[0], pos[1]), w_all.shape[1] // 8, w_all, sems
        )
        for copy in copies:
            copy.start()
        for copy in copies:
            copy.wait()
        for g in range(2):
            w_out[g] = w_all[g, :, width:]
        bias_out[...] = jnp.zeros_like(bias_out)

    grad = jnp.where(b < 2, g_own[...], g_other[...]).reshape(BLOCK, -1)
    piece = width // 3
    count = piece // HEAD_DIM
    log_sums = lse[0, 0].reshape(BLOCK, 2 * count)
    total = None
    for g in range(2):
        joined = qkv[g, 0].reshape(BLOCK, width)
        pulled = nn(grad, w_out[g]).astype(BF)
        found = [[], [], []]
        for n in range(count):
            at = n * HEAD_DIM
            query = joined[:, at : at + HEAD_DIM]
            keys = joined[:, piece + at : piece + at + HEAD_DIM]
            values = joined[:, 2 * piece + at : 2 * piece + at + HEAD_DIM]
            pull = pulled[:, at : at + HEAD_DIM]
            scores = nt(query, keys) * HEAD_DIM**-0.5
            if across:
                scores = jnp.where(masked(scores), scores, -1e30)
            probs = jnp.exp(scores - log_sums[:, g * count + n : g * count + n + 1])
            grad_probs = nt(pull, values)
            mean_term = jnp.sum(grad_probs * probs, axis=-1, keepdims=True)
            grad_scores = (probs * (grad_probs - mean_term)).astype(BF)
            found[0].append(nn(grad_scores, keys) * HEAD_DIM**-0.5)
            found[1].append(tn(grad_scores, query) * HEAD_DIM**-0.5)
            found[2].append(tn(probs.astype(BF), pull))
        triple = jnp.concatenate(found[0] + found[1] + found[2], axis=1).astype(BF)
        dqkv_out[g, 0] = triple.reshape(16, 16, width)
        bias_out[g] += column_sum(triple.astype(F32))
        term = nt(triple, w_all[g, :, :width])
        total = term if total is None else total + term
    total = total.astype(BF).reshape(16, 16, -1)

    @pl.when(b < 2)
    def _():
        own_out[...] = total

    @pl.when(b >= 2)
    def _():
        other_out[...] = total


def attend_back_call(pos, g_own, g_other, qkv, lse, weights, orders, across):
    width = g_own.shape[-1]
    wide = qkv.shape[-1]
    piece = wide // 3
    lead = viewed(across)
    smem = pl.BlockSpec(memory_space=pltpu.SMEM)
    heads = 2 * piece // HEAD_DIM
    flops = 2 * 4 * BLOCK * width * 2 * 4 * piece + 4 * heads * 10 * BLOCK * BLOCK * 128
    lse_spec = pl.BlockSpec(
        (1, 1, 16, 16, heads),
        lambda b: (0, b // 2, 0, b % 2, 0) if across else (0, b // 2, b % 2, 0, 0),
    )
    return pl.pallas_call(
        functools.partial(attend_back_kernel, across, orders),
        grid=(4,),
        in_specs=[
            smem,
            half_spec(width, across, 0),
            half_spec(width, across, 1),
            group_spec(wide, across),
            lse_spec,
        ]
        + [ANY_SPEC] * len(weights),
        out_specs=[
            group_spec(wide, across),
            half_spec(width, across, 0),
            half_spec(width, across, 1),
            whole_spec(2, 1, wide),
        ],
        out_shape=[
            shape_of((2, 2) + lead + (wide,), BF),
            shape_of(lead + (width,), BF),
            shape_of(lead + (width,), BF),
            shape_of((2, 1, wide), F32),
        ],
        scratch_shapes=[
            pltpu.VMEM((2, width, wide + piece), BF),
            pltpu.VMEM((2, width, piece), BF),
            pltpu.SemaphoreType.DMA((64,)),
        ],
        compiler_params=params(),
        cost_estimate=cost(flops, 20 * 2**20, 4 * heads * BLOCK * BLOCK),
    )(pos, g_own.reshape(lead + (width,)), g_other.reshape(lead + (width,)), qkv, lse, *weights)


def pick_spec(width, which):
    def index(b):
        return (jnp.minimum(b, 1) if which == 0 else jnp.maximum(b - 2, 0), 0)

    return pl.BlockSpec((BLOCK, width), index)


def hidden_spec(width):
    return pl.BlockSpec((2, BLOCK, width), lambda b: (0, b, 0))


def load_two(b, pos, up, down, orders_up, orders_down, w_up, w_down, sems):
    @pl.when(b == 0)
    def _():
        place = (pos[0], pos[1])
        rows = w_up.shape[1] // 8
        copies = weight_copies(up, orders_up, place, rows, w_up, sems.at[0])
        copies += weight_copies(down, orders_down, place, rows, w_down, sems.at[1])
        for copy in copies:
            copy.start()
        for copy in copies:
            copy.wait()


def expand_kernel(orders_up, orders_down, pos, *refs):
    n_up, n_down = 2 * len(orders_up), 2 * len(orders_down)
    u_own, u_other, bias = refs[:3]
    up, down, refs = refs[3 : 3 + n_up], refs[3 + n_up : 3 + n_up + n_down], refs[3 + n_up + n_down :]
    g_out, slope_out, own_out, other_out = refs[:4]
    w_up, w_down, sems = refs[4:]
    b = pl.program_id(0)
    load_two(b, pos, up, down, orders_up, orders_down, w_up, w_down, sems)
    u = jnp.where(b < 2, u_own[...], u_other[...])
    total = None
    for g in range(2):
        hidden = nn(u, w_up[g]) + bias[g]
        inner = 0.7978845608028654 * (hidden + 0.044715 * hidden * hidden * hidden)
        tangent = jnp.tanh(inner)
        active = (0.5 * hidden * (1.0 + tangent)).astype(BF)
        g_out[g] = active
        slope = 0.5 * (1.0 + tangent) + 0.5 * hidden * (1.0 - tangent * tangent) * (
            0.7978845608028654 * (1.0 + 3.0 * 0.044715 * hidden * hidden)
        )
        slope_out[g] = slope.astype(BF)
        term = nt(active, w_down[g])
        total = term if total is None else total + term
    total = total.astype(BF)

    @pl.when(b < 2)
    def _():
        own_out[...] = total

    @pl.when(b >= 2)
    def _():
        other_out[...] = total


def expand_call(pos, u_own, u_other, bias, up, down, orders_up, orders_down):
    width = u_own.shape[-1]
    units = bias.shape[-1]
    smem = pl.BlockSpec(memory_space=pltpu.SMEM)
    return pl.pallas_call(
        functools.partial(expand_kernel, orders_up, orders_down),
        grid=(4,),
        in_specs=[smem, pick_spec(width, 0), pick_spec(width, 1), whole_spec(2, 1, units)]
        + [ANY_SPEC] * (len(up) + len(down)),
        out_specs=[hidden_spec(units)] * 2 + [pick_spec(width, 0), pick_spec(width, 1)],
        out_shape=[
            shape_of((2, 2 * HALF, units), BF),
            shape_of((2, 2 * HALF, units), BF),
            shape_of((HALF, width), BF),
            shape_of((HALF, width), BF),
        ],
        scratch_shapes=[
            pltpu.VMEM((2, width, units), BF),
            pltpu.VMEM((2, width, units), BF),
            pltpu.SemaphoreType.DMA((2, 64)),
        ],
        compiler_params=params(),
        cost_estimate=cost(8 * 2 * HALF * width * units, 25 * 2**20, 4 * HALF * units),
    )(pos, u_own, u_other, bias, *up, *down)


def expand_back_kernel(orders_up, orders_down, pos, *refs):
    n_up, n_down = 2 * len(orders_up), 2 * len(orders_down)
    g_own, g_other, slope = refs[:3]
    up, down, refs = refs[3 : 3 + n_up], refs[3 + n_up : 3 + n_up + n_down], refs[3 + n_up + n_down :]
    dh_out, own_out, other_out, bias_out = refs[:4]
    w_up, w_down, sems = refs[4:]
    b = pl.program_id(0)
    load_two(b, pos, up, down, orders_up, orders_down, w_up, w_down, sems)

    @pl.when(b == 0)
    def _():
        bias_out[...] = jnp.zeros_like(bias_out)

    grad = jnp.where(b < 2, g_own[...], g_other[...])
    total = None
    for g in range(2):
        hidden = (nn(grad, w_down[g]) * slope[g].astype(F32)).astype(BF)
        dh_out[g] = hidden
        bias_out[g] += column_sum(hidden.astype(F32))
        term = nt(hidden, w_up[g])
        total = term if total is None else total + term
    total = total.astype(BF)

    @pl.when(b < 2)
    def _():
        own_out[...] = total

    @pl.when(b >= 2)
    def _():
        other_out[...] = total


def expand_back_call(pos, g_own, g_other, slope, up, down, orders_up, orders_down):
    width = g_own.shape[-1]
    units = slope.shape[-1]
    smem = pl.BlockSpec(memory_space=pltpu.SMEM)
    return pl.pallas_call(
        functools.partial(expand_back_kernel, orders_up, orders_down),
        grid=(4,),
        in_specs=[smem, pick_spec(width, 0), pick_spec(width, 1), hidden_spec(units)]
        + [ANY_SPEC] * (len(up) + len(down)),
        out_specs=[hidden_spec(units), pick_spec(width, 0), pick_spec(width, 1)]
        + [whole_spec(2, 1, units)],
        out_shape=[
            shape_of((2, 2 * HALF, units), BF),
            shape_of((HALF, width), BF),
            shape_of((HALF, width), BF),
            shape_of((2, 1, units), F32),
        ],
        scratch_shapes=[
            pltpu.VMEM((2, width, units), BF),
            pltpu.VMEM((2, width, units), BF),
            pltpu.SemaphoreType.DMA((2, 64)),
        ],
        compiler_params=params(),
        cost_estimate=cost(8 * 2 * HALF * width * units, 25 * 2**20),
    )(pos, g_own, g_other, slope, *up, *down)


def weight_grad_kernel(joint, order, pos, *refs):
    if joint:
        left, right, left_two, right_two = (refs[:2], refs[2], refs[3:5], refs[5])
        refs = refs[6:]
    else:
        left, right = refs[:2], refs[2]
        refs = refs[3:]
    outs, refs = refs[:2], refs[2:]
    stage, turned, sems = refs[0], refs[1], refs[-1]
    g, part = pl.program_id(0), pl.program_id(1)
    first = jnp.logical_and(g == 0, part == 0)
    last = jnp.logical_and(g == 1, part == 2)
    rows = turned.shape[0] // 8

    @pl.when(first)
    def _():
        for half in range(2):
            turned[:, half * HALF : (half + 1) * HALF] = left[half][...].T

    slot = g * 3 + part
    if joint:
        turned_two = refs[2]

        @pl.when(first)
        def _():
            for half in range(2):
                turned_two[:, half * HALF : (half + 1) * HALF] = left_two[half][...].T

        @pl.when(part < 2)
        def _():
            stage[slot] = nn(turned[...], right[0]).astype(BF)

        @pl.when(part == 2)
        def _():
            rest = PART - right_two.shape[-1]
            stage[slot] = jnp.concatenate(
                [nn(turned[...], right[0, :, :rest]), nn(turned_two[...], right_two[0])], axis=1
            ).astype(BF)
    else:
        stage[slot] = nn(turned[...], right[0]).astype(BF)

    def copies(group, index):
        made = []
        for y, high, low in itertools.product(range(2), repeat=3):
            at = {"x": group, "y": y, "a": low, "b": high}
            start = (((2 * high + low) ^ pos[0]) * 2 + (y ^ pos[1])) * rows
            one, two, three, four = (at[axis] for axis in order)
            made.append(
                pltpu.make_async_copy(
                    stage.at[group * 3 + index, pl.ds(pl.multiple_of(start, 16), rows)],
                    outs[one].at[two, three, four, :, pl.ds(index * PART, PART)],
                    sems.at[group * 3 + index, len(made)],
                )
            )
        return made

    for group in range(2):
        for index in range(3):

            @pl.when(jnp.logical_and(g == group, part == index))
            def _():
                for copy in copies(group, index):
                    copy.start()

    @pl.when(last)
    def _():
        for group in range(2):
            for index in range(3):
                for copy in copies(group, index):
                    copy.wait()


def weight_grad(pos, order, left, right, left_two=None, right_two=None):
    width = left[0].shape[-1]
    joint = left_two is not None
    smem = pl.BlockSpec(memory_space=pltpu.SMEM)

    def whole(*shape):
        return pl.BlockSpec(shape, lambda g, p: (0,) * len(shape))

    in_specs = [smem, whole(HALF, width), whole(HALF, width)]
    in_specs.append(pl.BlockSpec((1, 2 * HALF, PART), lambda g, p: (g, 0, p)))
    args = [pos, left[0], left[1], right]
    scratch = [pltpu.VMEM((6, width, PART), BF), pltpu.VMEM((width, 2 * HALF), BF)]
    if joint:
        in_specs += [whole(HALF, width), whole(HALF, width)]
        in_specs.append(
            pl.BlockSpec((1, 2 * HALF, right_two.shape[-1]), lambda g, p: (g, 0, 0))
        )
        args += [left_two[0], left_two[1], right_two]
        scratch.append(pltpu.VMEM((width, 2 * HALF), BF))
    return pl.pallas_call(
        functools.partial(weight_grad_kernel, joint, order),
        grid=(2, 3),
        in_specs=in_specs,
        out_specs=[ANY_SPEC] * 2,
        out_shape=[shape_of((2, 2, 2, width // 8, 3 * PART), BF)] * 2,
        scratch_shapes=scratch + [pltpu.SemaphoreType.DMA((6, 8))],
        compiler_params=params(2),
        cost_estimate=cost(2 * 2 * HALF * width * 6 * PART, 16 * 2**20),
    )(*args)


def spread_result_kernel(pos, *refs):
    pieces, out = refs[:8], refs[8]
    for source in range(4):
        for e in range(2):
            block = pos[3] ^ (4 * e + source)
            value = pieces[source * 2 + e][0]
            step = value.shape[1]
            out[:, pl.ds(pl.multiple_of(block * step, step), step), :] = value.astype(F32)


def spread_result(pos, pieces, places):
    _, pair, step, width = pieces[0].shape

    def spec(source):
        return pl.BlockSpec((1, pair, step, width), lambda t, p: (p[2] ^ source ^ t, 0, 0, 0))

    return pl.pallas_call(
        spread_result_kernel,
        grid_spec=pltpu.PrefetchScalarGridSpec(
            num_scalar_prefetch=1,
            grid=(4,),
            in_specs=[spec(source) for source in range(4) for _ in range(2)],
            out_specs=pl.BlockSpec((pair, places, width), lambda t, p: (t, 0, 0)),
        ),
        out_shape=shape_of((4 * pair, places, width), F32),
        compiler_params=params(),
        cost_estimate=cost(8 * HALF * width, 24 * HALF * width),
    )(pos, *pieces)


def spread_tokens_kernel(pos, *refs):
    pieces, out = refs[:4], refs[4]
    for source in range(4):

        @pl.when(pl.program_id(0) == source)
        def _():
            for r in range(8):
                block = pos[3] ^ source ^ r
                step = pieces[source].shape[2]
                out[:, pl.ds(pl.multiple_of(block * step, step), step), :] = pieces[source][
                    :, r
                ].astype(F32)


def spread_tokens(pos, pieces):
    pair, count, step, width = pieces[0].shape
    return pl.pallas_call(
        spread_tokens_kernel,
        grid_spec=pltpu.PrefetchScalarGridSpec(
            num_scalar_prefetch=1,
            grid=(4,),
            in_specs=[pl.BlockSpec((pair, count, step, width), lambda s, p: (0, 0, 0, 0))] * 4,
            out_specs=pl.BlockSpec(
                (pair, count * step, width), lambda s, p: (p[2] ^ s, 0, 0)
            ),
        ),
        out_shape=shape_of((4 * pair, count * step, width), F32),
        compiler_params=params(),
        cost_estimate=cost(8 * HALF * width, 24 * HALF * width),
    )(pos, *pieces)


def take_grad_kernel(pos, own, other, own_out, other_out):
    own_out[0] = own[...].astype(BF)
    other_out[0] = other[...].astype(BF)


def take_grad(pos, out_grad):
    _, places, width = out_grad.shape
    step = places // 8
    return pl.pallas_call(
        take_grad_kernel,
        grid_spec=pltpu.PrefetchScalarGridSpec(
            num_scalar_prefetch=1,
            grid=(4,),
            in_specs=[
                pl.BlockSpec((2, step, width), lambda j, p: (p[2] ^ j, p[3], 0)),
                pl.BlockSpec((2, step, width), lambda j, p: (p[2] ^ j, p[3] ^ 4, 0)),
            ],
            out_specs=[pl.BlockSpec((1, 2, step, width), lambda j, p: (j, 0, 0, 0))] * 2,
        ),
        out_shape=[shape_of((4, 2, step, width), BF)] * 2,
        compiler_params=params(),
        cost_estimate=cost(HALF * width, 6 * HALF * width),
    )(pos, out_grad, out_grad)


def pick(array, index):
    return lax.dynamic_index_in_dim(array, index, 0, keepdims=False)


def fast_body(
    tokens, condition, w_qkv, b_qv, w_out, b_out, w_up, b_up, w_down, b_down, w_mod, b_mod, out_grad
):
    z, y, hd = lax.axis_index("clip"), lax.axis_index("frame"), lax.axis_index("head")
    idx = 4 * y + hd
    pos = jnp.stack([z, y, hd, idx]).astype(jnp.int32)
    layers = w_qkv.shape[0]
    rows, piece, units = w_qkv.shape[1], w_qkv.shape[3], w_up.shape[2]
    width = tokens.shape[3]

    activated = jax.nn.silu(condition)
    partial = jnp.einsum("cd,ldje->clje", activated, w_mod, precision=highest)
    mine = jnp.stack([pick(partial, z), pick(partial, z ^ 1)])
    mine = mine + swap_z(jnp.stack([pick(partial, z ^ 2), pick(partial, z ^ 3)]), 2)
    mine = mine[0] + swap_z(mine[1], 1)
    mine = mine + swap_y(mine)
    pair = jnp.stack([mine, swap_core(mine)])
    quarters = jnp.concatenate([pair, swap_x(pair)])
    mod = jnp.concatenate([pick(quarters, hd ^ q) for q in range(4)], axis=-1) + b_mod
    vectors = jnp.concatenate([mod, b_out[:, None], b_down[:, None]], axis=1)

    bias_rows = jnp.concatenate([b_qv.reshape(layers, -1), b_up], axis=1)
    bias_rows = jnp.stack([bias_rows, swap_x(bias_rows)])
    zeros = jnp.zeros((2, layers, piece), F32)
    bias_qkv = jnp.concatenate(
        [bias_rows[:, :, :piece], zeros, bias_rows[:, :, piece : 2 * piece]], axis=2
    )[:, :, None]
    bias_up = bias_rows[:, :, None, 2 * piece :]

    buffers, orders = [], []
    for l in range(layers):
        low = [
            jnp.concatenate([w_qkv[l].reshape(rows, 3 * piece), w_out[l].T], axis=1).astype(BF),
            w_up[l].astype(BF),
            w_down[l].T.astype(BF),
        ]
        for shard in low:
            orders.append(GATHERS[len(orders)])
            buffers.append(gather_buffer(shard, orders[-1]))

    grad_own, grad_send = take_grad(pos, out_grad[0])
    grad_other = swap_y(grad_send)

    saved = []
    pieces = None
    for l in range(layers):
        across = l == 1
        b_attn, b_up_w, b_down_w = buffers[3 * l : 3 * l + 3]
        o_attn, o_up, o_down = orders[3 * l : 3 * l + 3]
        if l == 0:
            x, u = first_norm(pos, tokens[0], vectors[0])
            x, u = x.reshape(HALF, width), u.reshape(HALF, width)
        else:
            x, u = later_norm(pieces, vectors[l])
        u_other = swap_core(u)
        qkv, o, lse, a_own, a_send = attend_call(
            pos, u, u_other, bias_qkv[:, l], b_attn, o_attn, across
        )
        a_own = a_own.reshape(HALF, width)
        a_other = swap_core(a_send.reshape(HALF, width))
        x1, u2 = middle_call(x, a_own, a_other, vectors[l])
        u2_other = swap_core(u2)
        active, slope, m_own, m_send = expand_call(
            pos, u2, u2_other, bias_up[:, l], b_up_w, b_down_w, o_up, o_down
        )
        m_other = swap_core(m_send)
        ended = end_call(x1, m_own, m_other, vectors[l], across)
        if not across:
            pieces = [ended[0]] + [swap_clip(ended[r], r) for r in range(1, 8)]
        saved.append(
            (x, u, u_other, qkv, o, lse, a_own, a_other, x1, u2, u2_other, active, slope)
            + (m_own, m_other)
        )

    halves = [value.reshape(4, 2, 32, width) for value in ended]
    pair = [halves[0], swap_y(halves[1])]
    pair_x = [swap_x(value) for value in pair]
    sources = [pair, [swap_core(v) for v in pair], pair_x, [swap_core(v) for v in pair_x]]
    result = spread_result(pos, [v for s in sources for v in s], tokens.shape[2])

    grads = [grad_own.reshape(BLOCK, width), grad_other.reshape(BLOCK, width)]
    sums, bias_sums, shards = [None] * layers, [None] * layers, [None] * layers
    for l in reversed(range(layers)):
        across = l == 1
        b_attn, b_up_w, b_down_w = buffers[3 * l : 3 * l + 3]
        o_attn, o_up, o_down = orders[3 * l : 3 * l + 3]
        (x, u, u_other, qkv, o, lse, a_own, a_other, x1, u2, u2_other, active, slope) = saved[l][
            :13
        ]
        m_own, m_other = saved[l][13:]
        e, em, sums_one = before_call(grads, m_own, m_other, vectors[l], across)
        em_other = swap_core(em)
        d_down = weight_grad(pos, SCATTERS[3 * l + 2], (em, em_other), active)
        dh, d_own, d_send, up_sum = expand_back_call(
            pos, em, em_other, slope, b_up_w, b_down_w, o_up, o_down
        )
        d_other = swap_core(d_send)
        d_up = weight_grad(pos, SCATTERS[3 * l + 1], (u2, u2_other), dh)
        e1, ea, sums_two = between_call(d_own, d_other, x1, e, a_own, a_other, vectors[l])
        ea_other = swap_core(ea)
        dqkv, d_own, d_send, qkv_sum = attend_back_call(
            pos, ea, ea_other, qkv, lse, b_attn, o_attn, across
        )
        d_other = swap_core(d_send.reshape(HALF, width))
        d_attn = weight_grad(
            pos,
            SCATTERS[3 * l],
            (u, u_other),
            dqkv.reshape(2, 2 * HALF, 3 * piece),
            (ea, ea_other),
            o.reshape(2, 2 * HALF, piece),
        )
        *ended, sums_three = after_call(
            d_own.reshape(HALF, width), d_other, x, e1, vectors[l], across
        )
        if across:
            grads = [ended[0]] + [swap_clip(ended[r], r) for r in range(1, 8)]
        sums[l] = sums_one + sums_two + sums_three
        bias_sums[l] = jnp.concatenate(
            [qkv_sum[:, 0, :piece], qkv_sum[:, 0, 2 * piece :], up_sum[:, 0]], axis=1
        )
        shards[l] = [
            scatter_buffer(outs, SCATTERS[3 * l + i])
            for i, outs in enumerate((d_attn, d_up, d_down))
        ]

    own = ended[0].reshape(2, 8, 32, width)
    own_x = swap_x(own)
    tokens_grad = spread_tokens(pos, [own, swap_core(own), own_x, swap_core(own_x)])

    clip_sums = jnp.stack(sums)
    kept = jnp.stack([b[0] for b in bias_sums])
    sent = jnp.stack([b[1] for b in bias_sums])
    count = clip_sums.size

    def flat(*values):
        return jnp.concatenate([v.reshape(-1) for v in values])

    total = flat(clip_sums, kept) + swap_x(flat(clip_sums, sent))
    total = total + swap_y(total)
    clip_part = total[:count].reshape(clip_sums.shape)
    clip_part = clip_part + swap_core(clip_part)
    total = flat(clip_part, total[count:])
    clips = [total, swap_z(total, 1)]
    clips += list(swap_z(jnp.stack(clips), 2))
    bias_total = sum(c[count:] for c in clips).reshape(kept.shape)
    by_clip = jnp.stack([c[:count].reshape(clip_sums.shape) for c in clips])
    all_clips = jnp.sum(by_clip, axis=0)
    b_mod_grad = all_clips[:, :6]
    b_out_grad, b_down_grad = all_clips[:, 6], all_clips[:, 7]
    b_qv_grad = bias_total[:, : 2 * piece].reshape(layers, 2, piece)
    b_up_grad = bias_total[:, 2 * piece :]

    columns = lax.dynamic_slice_in_dim(by_clip[:, :, :6], hd * piece, piece, 3)
    near = jnp.stack([pick(activated, z ^ k) for k in range(4)])
    w_mod_grad = sum(
        near[k][None, :, None, None] * columns[k][:, None] for k in range(4)
    )
    cond_part = jnp.einsum("clje,ldje->cd", columns, w_mod, precision=highest)
    cond_part = jnp.stack([pick(cond_part, z ^ k) for k in range(4)])
    cond_part = cond_part + swap_x(cond_part)
    cond_part = cond_part + swap_core(cond_part)
    sigma = jax.nn.sigmoid(condition)
    cond_grad = cond_part * sigma * (1.0 + condition * (1.0 - sigma))

    w_qkv_grad = jnp.stack(
        [s[0][:, : 3 * piece].reshape(rows, 3, piece) for s in shards]
    )
    w_out_grad = jnp.stack([s[0][:, 3 * piece :].T for s in shards])
    w_up_grad = jnp.stack([s[1] for s in shards])
    w_down_grad = jnp.stack([s[2].T for s in shards])
    return (
        result[None],
        tokens_grad[None],
        cond_grad,
        w_qkv_grad,
        b_qv_grad,
        w_out_grad,
        b_out_grad,
        w_up_grad,
        b_up_grad,
        w_down_grad,
        b_down_grad,
        w_mod_grad,
        b_mod_grad,
    )


def solution(mesh):
    sizes = dict(mesh.shape)
    fits = (sizes["clip"], sizes["frame"], sizes["head"]) == (4, 2, 4)
    return jax.shard_map(
        fast_body if fits else body,
        mesh=mesh,
        in_specs=(
            P("clip", "frame", None, None),
            P(None, ("clip", "frame")),
            P(None, ("clip", "frame"), None, "head"),
            P(None, None, "head"),
            P(None, "head", ("clip", "frame")),
            P(),
            P(None, ("clip", "frame"), "head"),
            P(None, "head"),
            P(None, "head", ("clip", "frame")),
            P(),
            P(None, ("clip", "frame"), None, "head"),
            P(),
            P("clip", "frame", None, None),
        ),
        out_specs=(
            P("clip", "frame", None, None),
            P("clip", "frame", None, None),
            P(None, ("clip", "frame")),
            P(None, ("clip", "frame"), None, "head"),
            P(None, None, "head"),
            P(None, "head", ("clip", "frame")),
            P(),
            P(None, ("clip", "frame"), "head"),
            P(None, "head"),
            P(None, "head", ("clip", "frame")),
            P(),
            P(None, ("clip", "frame"), None, "head"),
            P(),
        ),
        check_vma=False,
    )
```
